256 devices in a mesh: net: 32 (over x, z), scen: 8 (over y, core).
Axes of the slice: x: 4, y: 4, z: 8, core: 2. Of those that a mesh axis runs over, the one named last changes fastest.
Arguments:
- arc_flows: float32 [256, 262144], P('scen', 'net'), may hold values from 0 to 1
- node_duals: float32 [256, 65536], P('scen', 'net'), may hold values from -6 to 6
- demand: float32 [256, 65536], P('scen', 'net'), may hold values from -6 to 6
- excess: float32 [256], P('scen'), may hold values from 0 to 0.5
- risk_duals: float32 [256], P('scen'), may hold values from 0.2 to 6
- threshold: float32 [1], replicated, may hold values from -2.5 to -1.5
- arc_costs: float32 [262144], P('net'), may hold values from 0.05 to 0.75
- local_blocks: bfloat16 [2048, 4, 128, 128], P('net'), may hold values from -0.125 to 0.125
- head_blocks: bfloat16 [2048, 128, 128], P('net'), may hold values from -0.125 to 0.125
- local_index: int32 [2048, 4], P('net'), may hold values from 0 to 15
- head_index: int32 [2048], P('net'), may hold values from 0 to 511, as said below
Outputs:
- flows_next: float32 [256, 262144], P('scen', 'net')
- duals_next: float32 [256, 65536], P('scen', 'net')
- excess_next: float32 [256], P('scen')
- risk_next: float32 [256], P('scen')
- threshold_next: float32 [1], replicated
The draws below stay inside these ranges and needn't reach their ends.
Inputs may be any that keep to these rules, and one draw needn't show every extreme that they name: Among the arc blocks of one device, at most 4 have their head node block on any one device of net (head_index // 16 names the device), and in every device's arc blocks some device of net is named exactly 4 times.
All inputs are finite; a program needn't handle non-finite values.
Results may differ from the reference program's by a relative error of at most 0.0021.
Values may be sent and summed in bfloat16 or wider, within the bound.
A program may use at most 128 MiB of HBM per device.

```python
import math
import jax
import jax.numpy as jnp

BLOCK_ROWS = 128
NODE_BLKS = 16
ARC_BLKS = 64
TOUCHES = 4
ROUNDS = 3
SCENARIOS = 256
ARC_BLOCKS = 2048
NODE_BLOCKS = 512
ARC_COUNT = 262144
NODE_COUNT = 65536
SLOT_CAP = 4


def draw_head_index(key, part):
    devices = ARC_BLOCKS // ARC_BLKS
    slot_count = devices * SLOT_CAP

    def draw_device(device):
        folded = jax.random.fold_in(key, device)
        subkeys = jax.random.split(folded, 4)
        ordering = jax.random.permutation(subkeys[0], slot_count)
        favored = jax.random.randint(subkeys[1], (), 0, devices)
        places = jnp.arange(slot_count, dtype=jnp.int32)
        scores = jnp.where(ordering // SLOT_CAP == favored, places, places + slot_count)
        ranked = ordering[jnp.argsort(scores)]
        chosen = ranked[:ARC_BLKS]
        chosen = chosen[jax.random.permutation(subkeys[2], ARC_BLKS)]
        inside = jax.random.randint(subkeys[3], (ARC_BLKS,), 0, NODE_BLKS)
        return chosen // SLOT_CAP * NODE_BLKS + inside
    return jax.vmap(draw_device)(jnp.arange(devices)).reshape(-1).astype(jnp.int32)


def draw_arc_costs(key, part):
    rising = 1.0 + 2.0 * jnp.arange(ARC_COUNT).astype(jnp.float32) / ARC_COUNT
    uniform_draw = jax.random.uniform(key, (ARC_COUNT,), jnp.float32)
    levels = 0.05 * jnp.exp(uniform_draw * math.log(5.0))
    return (levels * rising).astype(jnp.float32)


def draw_risk_duals(key, part):
    rising = 1.0 + 2.0 * jnp.arange(SCENARIOS).astype(jnp.float32) / SCENARIOS
    uniform_draw = jax.random.uniform(key, (SCENARIOS,), jnp.float32)
    levels = 0.2 + 1.8 * uniform_draw
    return (levels * rising).astype(jnp.float32)


def place_ends(result, rng, low, high):
    spot = [jax.random.randint(jax.random.fold_in(rng, axis), (), 0, length) for axis, length in enumerate(result.shape)]
    main_axis = result.shape.index(max(result.shape))
    beside = spot[:main_axis] + [(spot[main_axis] + 1) % result.shape[main_axis]] + spot[main_axis + 1:]
    return result.at[tuple(spot)].set(low).at[tuple(beside)].set(high)


def shard_levels(own_key, extent, pieces, low, top_value):
    loudness, own = 1.0, jax.random.fold_in(own_key, 6)
    for position, parts in pieces:
        heights = jnp.exp(jax.random.uniform(jax.random.fold_in(own, position), (parts,), jnp.float32, low / len(pieces), top_value / len(pieces)))
        loudness = loudness * jnp.repeat(heights, extent[position] // parts).reshape([-1 if axis == position else 1 for axis in range(len(extent))])
    return loudness


def centred(own_key, extent, spread, reach, pieces=(), kind=jnp.bfloat16):
    level = shard_levels(own_key, extent, pieces, -0.22, 0.18) if pieces else 1.0
    drawn = jax.random.normal(own_key, extent, jnp.float32) * spread * level
    return jnp.minimum(jnp.maximum(drawn, -reach), reach).astype(kind)


def setup_inputs(seed: int = 0) -> dict:
    streams_of = jax.random.split(jax.random.key(seed), 12)
    arc_flows = jnp.clip(1.0 * jax.random.uniform(streams_of[0], (SCENARIOS, ARC_COUNT), jnp.float32) ** shard_levels(streams_of[0], (SCENARIOS, ARC_COUNT), ((0, 8), (1, 32)), -0.2, 0.2), 0.0, 1.0)
    node_duals = centred(streams_of[1], (SCENARIOS, NODE_COUNT), 1.0, 6.0, ((0, 8), (1, 32)), jnp.float32)
    demand = centred(streams_of[2], (SCENARIOS, NODE_COUNT), 1.0, 6.0, ((0, 8), (1, 32)), jnp.float32)
    excess = jnp.clip(0.5 * jax.random.uniform(streams_of[3], (SCENARIOS,), jnp.float32) ** shard_levels(streams_of[3], (SCENARIOS,), ((0, 8),), -0.2, 0.2), 0.0, 0.5)
    risk_duals = draw_risk_duals(jax.random.fold_in(streams_of[11], 71), 0)
    threshold = jnp.clip(jax.random.uniform(streams_of[5], (1,), jnp.float32, -2.5, -1.5), -2.5, -1.5)
    arc_costs = draw_arc_costs(jax.random.fold_in(streams_of[11], 71), 0)
    local_blocks = centred(streams_of[7], (ARC_BLOCKS, TOUCHES, BLOCK_ROWS, BLOCK_ROWS), (BLOCK_ROWS * 4 * (TOUCHES + 1)) ** -0.5, 0.125, ((0, 32),))
    head_blocks = centred(streams_of[8], (ARC_BLOCKS, BLOCK_ROWS, BLOCK_ROWS), (BLOCK_ROWS * 4 * (TOUCHES + 1)) ** -0.5, 0.125, ((0, 32),))
    local_index = place_ends(jax.random.randint(streams_of[9], (ARC_BLOCKS, TOUCHES), 0, NODE_BLKS), jax.random.fold_in(streams_of[9], 1), 0, NODE_BLKS - 1).astype(jnp.int32)
    head_index = draw_head_index(jax.random.fold_in(streams_of[11], 71), 0)
    return dict(arc_flows=arc_flows, node_duals=node_duals, demand=demand, excess=excess, risk_duals=risk_duals, threshold=threshold, arc_costs=arc_costs, local_blocks=local_blocks, head_blocks=head_blocks, local_index=local_index, head_index=head_index)


primal_step = 0.5
dual_step = 0.5
risk_step = 1.0
tail_weight = 2.0


def apply_forward(flow_panel, local_blocks, head_blocks, node_ids, head_index):
    scen_rows = flow_panel.shape[0]
    arc_panel = flow_panel.astype(jnp.float32).reshape(scen_rows, ARC_BLOCKS, BLOCK_ROWS)
    summed = jnp.zeros((scen_rows, NODE_BLOCKS, BLOCK_ROWS), jnp.float32)
    products = jnp.einsum("sjm,jmn->sjn", arc_panel, head_blocks.astype(jnp.float32))
    summed = summed.at[:, head_index, :].add(products)
    for touched in range(TOUCHES):
        products = jnp.einsum("sjm,jmn->sjn", arc_panel, local_blocks[:, touched].astype(jnp.float32))
        summed = summed.at[:, node_ids[:, touched], :].add(products)
    return summed.reshape(scen_rows, NODE_COUNT)


def apply_adjoint(dual_panel, local_blocks, head_blocks, node_ids, head_index):
    scen_rows = dual_panel.shape[0]
    node_panel = dual_panel.astype(jnp.float32).reshape(scen_rows, NODE_BLOCKS, BLOCK_ROWS)
    head_rows = node_panel[:, head_index, :]
    summed = jnp.einsum("sjn,jmn->sjm", head_rows, head_blocks.astype(jnp.float32))
    for touched in range(TOUCHES):
        local_rows = node_panel[:, node_ids[:, touched], :]
        summed = summed + jnp.einsum("sjn,jmn->sjm", local_rows, local_blocks[:, touched].astype(jnp.float32))
    return summed.reshape(scen_rows, ARC_COUNT)


def reference(arc_flows, node_duals, demand, excess, risk_duals, threshold, arc_costs, local_blocks, head_blocks, local_index, head_index):
    owners = (jnp.arange(ARC_BLOCKS, dtype=jnp.int32) // ARC_BLKS) * NODE_BLKS
    node_ids = (owners[:, None] + local_index).astype(jnp.int32)
    flows = arc_flows
    duals = node_duals
    excess_now = excess
    risk = risk_duals
    level = threshold
    for iteration in range(ROUNDS):
        dual_panel = duals.astype(jnp.bfloat16)
        pulled = apply_adjoint(dual_panel, local_blocks, head_blocks, node_ids, head_index)
        flows_new = jnp.maximum(flows - primal_step * (risk[:, None] * arc_costs[None, :] - pulled), 0.0)
        excess_new = jnp.maximum(excess_now - primal_step * (tail_weight - risk), 0.0)
        level_new = level - primal_step * (1.0 - jnp.mean(risk))
        flows_bar = 2.0 * flows_new - flows
        excess_bar = 2.0 * excess_new - excess_now
        level_bar = 2.0 * level_new - level
        losses = jnp.mean(arc_costs[None, :] * flows_bar, axis=1)
        risk = jnp.maximum(risk + risk_step * (losses - excess_bar - level_bar), 0.0)
        flow_panel = flows_bar.astype(jnp.bfloat16)
        duals = duals + dual_step * (demand - apply_forward(flow_panel, local_blocks, head_blocks, node_ids, head_index))
        flows = flows_new
        excess_now = excess_new
        level = level_new
    return (flows, duals, excess_now, risk, level)
```

```python
import functools

import jax
import jax.numpy as jnp
from jax import lax
from jax.experimental import pallas as pl
from jax.experimental.pallas import tpu as pltpu
from jax.sharding import PartitionSpec as P

ROUNDS = 3
NZ = 8
SLOT = 4
PRIMAL = 0.5
DUAL = 0.5
RISK = 1.0
TAIL = 2.0
MESH = pl.DeviceIdType.MESH
NT = (((1,), (1,)), ((), ()))
F32 = jnp.float32
BF16 = jnp.bfloat16
ORDER = (4, 3, 5, 2, 6, 1, 7, 0)
GROUPS = ((0, 1), (1, 2), (3, 2), (5, 2), (7, 1))


def table_kernel(nx, node_blks, head_ref, index_ref, pos_ref, arc_ref, want_ref, prev_ref, last_ref, count):
    arc_blks, touches = index_ref.shape
    me = lax.axis_index("net")
    x, z = me // NZ, me % NZ
    slots = NZ * SLOT

    def clear(i, _):
        arc_ref[i] = 0
        want_ref[i // slots, i % slots] = node_blks
        return 0

    lax.fori_loop(0, nx * slots, clear, 0)

    def clear_count(i, _):
        count[i] = 0
        return 0

    lax.fori_loop(0, nx * NZ, clear_count, 0)

    def clear_last(b, _):
        last_ref[b] = arc_blks * touches
        return 0

    lax.fori_loop(0, node_blks, clear_last, 0)

    def place(j, _):
        head = head_ref[j]
        dev = head // node_blks
        e = (x - dev // NZ + nx) % nx
        o = (z - dev % NZ + NZ) % NZ
        w = jnp.where(o >= 4, 2 * (o - 4), 7 - 2 * o)
        rank = count[e * NZ + w]
        count[e * NZ + w] = rank + 1
        inside = w * SLOT + rank
        pos_ref[j] = e * slots + inside
        arc_ref[e * slots + inside] = j
        want_ref[e, inside] = head % node_blks
        for k in range(touches):
            b = index_ref[j, k]
            prev_ref[j * touches + k] = last_ref[b]
            last_ref[b] = j * touches + k
        return 0

    lax.fori_loop(0, arc_blks, place, 0)


def main_kernel(
    nx,
    ns,
    scen_total,
    arc_total,
    duals_hbm,
    flows_hbm,
    demand_ref,
    cost_ref,
    excess_in,
    risk_in,
    level_in,
    local_hbm,
    head_hbm,
    index_ref,
    pos_ref,
    arc_ref,
    want_ref,
    want_vec,
    prev_ref,
    last_ref,
    flows_ref,
    duals_ref,
    excess_out,
    risk_out,
    level_out,
    local_ref,
    head_ref,
    c0, c1, c2, c3, c4, c5, c6, c7,
    ask_vec,
    ask_ref,
    chain_prev,
    chain_last,
    pull_ref,
    panel_ref,
    term_ref,
    seg_ref,
    segx_ref,
    x_in,
    x_out,
    fx_in,
    fx_out,
    sl_ref,
    sr_ref,
    ll_ref,
    rr_ref,
    excess_ref,
    risk_ref,
    level_ref,
    lossx,
    lossz,
    scen_rows,
    load_sem,
    ask_send, ask_recv,
    ag_send, ag_recv,
    x_send, x_recv,
    f_send, f_recv,
    r_send, r_recv,
    lx_send, lx_recv,
    lz_send, lz_recv,
    sc_send, sc_recv,
):
    chunks = (c0, c1, c2, c3, c4, c5, c6, c7)
    arc_blks = pos_ref.shape[0]
    touches = local_ref.shape[1]
    rows = panel_ref.shape[1]
    blk = panel_ref.shape[2]
    node_blks = c0.shape[0]
    half = node_blks // 2
    me = lax.axis_index("net")
    scen = lax.axis_index("scen")
    x, z = me // NZ, me % NZ

    def x_peer(e):
        return {"net": lax.rem(x + e, nx) * NZ + z}

    def z_peer(d):
        return {"net": x * NZ + lax.rem(z + d, NZ)}

    def s_peer(d):
        return {"scen": lax.rem(scen + d, ns)}

    def remote(src, dst, send, recv, device):
        return pltpu.make_async_remote_copy(
            src_ref=src, dst_ref=dst, send_sem=send, recv_sem=recv, device_id=device, device_id_type=MESH
        )

    def columns(b):
        return pl.ds(pl.multiple_of(b * blk, blk), blk)

    def ag_copy(direction, step, h):
        n = step if direction == 0 else (NZ - step)
        src = chunks[step - 1] if direction == 0 else chunks[(NZ - step + 1) % NZ]
        part = pl.ds(h * half, half)
        i = direction * 8 + (step - 1) * 2 + h
        return remote(
            src.at[part], chunks[n].at[part], ag_send.at[i], ag_recv.at[i], z_peer(1 if direction == 0 else NZ - 1)
        )

    def x_copy(g, e):
        first, count = GROUPS[g]
        part = pl.ds(first * SLOT, count * SLOT)
        i = g * (nx - 1) + e - 1
        return remote(
            x_out.at[e - 1, part], x_in.at[e, part], x_send.at[i], x_recv.at[i], x_peer(e)
        )

    def f_copy(g, e):
        first, count = GROUPS[g]
        part = pl.ds(first * SLOT, count * SLOT)
        i = g * (nx - 1) + e - 1
        return remote(
            fx_out.at[e - 1, part], fx_in.at[e - 1, part], f_send.at[i], f_recv.at[i], x_peer(nx - e)
        )

    def rs_copy(direction, step, h):
        src = (sl_ref if direction == 0 else sr_ref).at[step - 1]
        dst = (ll_ref if direction == 0 else rr_ref).at[step - 1]
        part = pl.ds(h * half, half)
        i = direction * 8 + (step - 1) * 2 + h
        return remote(
            src.at[part], dst.at[part], r_send.at[i], r_recv.at[i], z_peer(NZ - 1 if direction == 0 else 1)
        )

    def lx_copy(r, e):
        i = r * (nx - 1) + e - 1
        return remote(lossx.at[r, x], lossx.at[r, x], lx_send.at[i], lx_recv.at[i], x_peer(e))

    def lz_copy(r, d):
        i = r * (NZ - 1) + d - 1
        return remote(lossz.at[r, z], lossz.at[r, z], lz_send.at[i], lz_recv.at[i], z_peer(d))

    def sc_copy(r, d):
        i = r * (ns - 1) + d - 1
        return remote(scen_rows.at[r, scen], scen_rows.at[r, scen], sc_send.at[i], sc_recv.at[i], s_peer(d))

    def ask_copy(e):
        return remote(
            want_vec.at[pl.ds(e, 1)], ask_vec.at[pl.ds(e, 1)], ask_send.at[e - 1], ask_recv.at[e - 1], x_peer(nx - e)
        )

    def start_ring():
        for h in range(2):
            ag_copy(0, 1, h).start()
            ag_copy(1, 1, h).start()

    load_duals = pltpu.make_async_copy(duals_hbm, duals_ref, load_sem.at[0])
    load_local = pltpu.make_async_copy(local_hbm, local_ref, load_sem.at[1])
    load_flows = pltpu.make_async_copy(flows_hbm, flows_ref, load_sem.at[2])
    load_heads = pltpu.make_async_copy(head_hbm, head_ref, load_sem.at[3])
    load_duals.start()
    load_local.start()
    load_flows.start()
    load_heads.start()
    barrier = pltpu.get_barrier_semaphore()
    peers = (
        [x_peer(e) for e in range(1, nx)] + [z_peer(d) for d in range(1, NZ)] + [s_peer(d) for d in range(1, ns)]
    )
    for peer in peers:
        pl.semaphore_signal(barrier, inc=1, device_id=peer, device_id_type=MESH)
    lane = lax.broadcasted_iota(jnp.int32, (rows, blk), 1)
    diagonal = lax.broadcasted_iota(jnp.int32, (rows, blk), 0) == lane
    real = lax.broadcasted_iota(jnp.int32, (1, blk), 1) < rows
    excess_ref[...] = jnp.zeros_like(excess_ref)
    risk_ref[...] = jnp.zeros_like(risk_ref)
    excess_ref[:, 0:rows] = excess_in[...]
    risk_ref[:, 0:rows] = risk_in[...]
    level_ref[...] = jnp.broadcast_to(level_in[...], level_ref.shape)
    seg_ref[arc_blks * touches] = jnp.zeros((rows, blk), F32)
    segx_ref[0] = jnp.zeros((rows, blk), F32)
    load_duals.wait()
    for b in range(node_blks):
        c0[b] = duals_ref[:, b * blk : (b + 1) * blk].astype(BF16)
    pl.semaphore_wait(barrier, len(peers))
    for e in range(1, nx):
        ask_copy(e).start()
    start_ring()

    for e in range(1, nx):
        ask_copy(e).wait_recv()
    to_scalar = pltpu.make_async_copy(ask_vec, ask_ref, load_sem.at[4])
    to_scalar.start()
    to_scalar.wait()
    for e in range(1, nx):
        ask_copy(e).wait_send()

    def asked(e, s):
        return want_ref[0, s] if e == 0 else ask_ref[e, s]

    def chain_tables(w, _):
        named = [asked(q // SLOT, w * SLOT + q % SLOT) for q in range(nx * SLOT)]
        for q in range(nx * SLOT):
            found = jnp.int32(0)
            for p in range(q):
                found = jnp.where(named[p] == named[q], w * (nx * SLOT) + p + 1, found)
            chain_prev[w * (nx * SLOT) + q] = found
        for b in range(node_blks):
            found = jnp.int32(0)
            for q in range(nx * SLOT):
                found = jnp.where(named[q] == b, w * (nx * SLOT) + q + 1, found)
            chain_last[w * node_blks + b] = found
        return 0

    lax.fori_loop(0, NZ, chain_tables, 0)
    load_local.wait()
    load_flows.wait()
    load_heads.wait()

    def pull_local(first, count):
        def body(i, _):
            j = first + i
            total = jnp.zeros((rows, blk), F32)
            for k in range(touches):
                total += lax.dot_general(
                    c0[index_ref[j, k]], local_ref[j, k], NT, preferred_element_type=F32
                )
            pull_ref[j] = total
            return 0

        lax.fori_loop(0, count, body, 0, unroll=4)

    def push_local(first, count):
        def body(i, _):
            j = first + i
            v = panel_ref[j]
            for k in range(touches):
                p = j * touches + k
                term = jnp.dot(v, local_ref[j, k], preferred_element_type=F32)
                seg_ref[p] = term + seg_ref[prev_ref[p]]
            return 0

        lax.fori_loop(0, count, body, 0, unroll=4)

    def answer(w):
        chunk = chunks[ORDER[w]]
        for e in range(nx):
            for s in range(SLOT):
                i = w * SLOT + s
                block = chunk[jnp.minimum(asked(e, i), node_blks - 1)]
                if e == 0:
                    x_in[0, i] = block
                else:
                    x_out[e - 1, i] = block

    def answer_group(g):
        first, count = GROUPS[g]
        for w in range(first, first + count):
            answer(w)
        for e in range(1, nx):
            x_copy(g, e).start()

    def collect(w):
        for q in range(nx * SLOT):
            e, i = q // SLOT, w * SLOT + q % SLOT
            value = term_ref[arc_ref[i]] if e == 0 else fx_in[e - 1, i]
            n = w * (nx * SLOT) + q
            segx_ref[n + 1] = value.astype(F32) + segx_ref[chain_prev[n]]

    def send_sum(direction, step, h, with_arrived):
        w = ORDER.index(5 - step if direction == 0 else 3 + step)
        dst = sl_ref if direction == 0 else sr_ref
        arrived = ll_ref if direction == 0 else rr_ref
        if with_arrived:
            rs_copy(direction, step - 1, h).wait_recv()
        for b in range(h * half, (h + 1) * half):
            value = segx_ref[chain_last[w * node_blks + b]]
            if with_arrived:
                value = value + arrived[step - 2, b].astype(F32)
            dst[step - 1, b] = value.astype(BF16)
        rs_copy(direction, step, h).start()

    def one_round(r, _):
        scen_rows[r, scen] = risk_ref[...]
        for d in range(1, ns):
            sc_copy(r, d).start()
        piece = arc_blks // 8
        answer_group(4)
        pull_local(0, 2 * piece)
        done = 2
        for step in range(1, 4):
            for h in range(2):
                ag_copy(0, step, h).wait_recv()
                if step < 3 or h == 0:
                    ag_copy(0, step + 1, h).start()
                ag_copy(1, step, h).wait_recv()
                if step < 3 or h == 1:
                    ag_copy(1, step + 1, h).start()
                if h == 1:
                    answer_group(4 - step)
                pull_local(done * piece, piece)
                done += 1
        ag_copy(0, 4, 0).wait_recv()
        ag_copy(1, 4, 1).wait_recv()
        answer_group(0)
        risk_wide = jnp.broadcast_to(
            jnp.sum(jnp.where(diagonal, jnp.broadcast_to(risk_ref[...], (rows, blk)), 0.0), axis=1, keepdims=True),
            (rows, blk),
        )
        for g in range(len(GROUPS)):
            for e in range(1, nx):
                x_copy(4 - g, e).wait_recv()

        def head(j, loss):
            pulled = pull_ref[j] + lax.dot_general(
                x_in[pos_ref[j] // (NZ * SLOT), pos_ref[j] % (NZ * SLOT)],
                head_ref[j],
                NT,
                preferred_element_type=F32,
            )
            cost = jnp.broadcast_to(cost_ref[pl.ds(j, 1), :], (rows, blk))
            now = flows_ref[:, columns(j)]
            new = jnp.maximum(now - PRIMAL * (risk_wide * cost - pulled), 0.0)
            bar = 2.0 * new - now
            flows_ref[:, columns(j)] = new
            panel = bar.astype(BF16)
            panel_ref[j] = panel
            term_ref[j] = jnp.dot(panel, head_ref[j], preferred_element_type=F32).astype(BF16)
            return loss + cost * bar

        loss = lax.fori_loop(0, arc_blks, head, jnp.zeros((rows, blk), F32), unroll=4)

        for g, (first, count) in enumerate(GROUPS):
            for e in range(1, nx):
                for i in range(first * SLOT, (first + count) * SLOT):
                    fx_out[e - 1, i] = term_ref[arc_ref[e * NZ * SLOT + i]]
                f_copy(g, e).start()
        wide = jnp.broadcast_to(jnp.sum(loss, axis=1, keepdims=True), (rows, blk))
        lossx[r, x] = jnp.sum(jnp.where(diagonal, wide, 0.0), axis=0, keepdims=True)
        for e in range(1, nx):
            lx_copy(r, e).start()
        for direction in range(2):
            for step in range(1, 5):
                for h in range(2):
                    if step < 4 or h == direction:
                        ag_copy(direction, step, h).wait_send()
        for g in range(len(GROUPS)):
            for e in range(1, nx):
                x_copy(g, e).wait_send()
        push_local(0, 2 * piece)

        for e in range(1, nx):
            f_copy(0, e).wait_recv()
        collect(0)
        send_sum(0, 1, 0, False)
        send_sum(1, 1, 1, False)
        for e in range(1, nx):
            lx_copy(r, e).wait_recv()
        total = lossx[r, 0]
        for i in range(1, nx):
            total = total + lossx[r, i]
        lossz[r, z] = total
        for d in range(1, NZ):
            lz_copy(r, d).start()
        done = 2
        for step in range(2, 5):
            for e in range(1, nx):
                f_copy(step - 1, e).wait_recv()
            collect(2 * step - 3)
            collect(2 * step - 2)
            for turn in range(2):
                send_sum(0, step, 1 - turn, step > 2 or turn == 1)
                send_sum(1, step, turn, step > 2 or turn == 1)
                push_local(done * piece, piece)
                done += 1
        for e in range(1, nx):
            f_copy(4, e).wait_recv()
        collect(7)

        for d in range(1, NZ):
            lz_copy(r, d).wait_recv()
        losses = lossz[r, 0]
        for i in range(1, NZ):
            losses = losses + lossz[r, i]
        losses = losses / arc_total
        for d in range(1, ns):
            sc_copy(r, d).wait_recv()
        risk_sum = scen_rows[r, 0]
        for i in range(1, ns):
            risk_sum = risk_sum + scen_rows[r, i]
        mean = jnp.broadcast_to(jnp.sum(risk_sum, axis=1, keepdims=True), (1, blk)) / scen_total
        risk = risk_ref[...]
        excess = excess_ref[...]
        level = level_ref[...]
        excess_new = jnp.maximum(excess - PRIMAL * (TAIL - risk), 0.0)
        level_new = level - PRIMAL * (1.0 - mean)
        excess_bar = 2.0 * excess_new - excess
        level_bar = 2.0 * level_new - level
        risk_new = jnp.maximum(risk + RISK * (losses - excess_bar - level_bar), 0.0)
        excess_ref[...] = excess_new
        level_ref[...] = level_new
        for d in range(1, ns):
            sc_copy(r, d).wait_send()
        for d in range(1, NZ):
            lz_copy(r, d).wait_send()
        for e in range(1, nx):
            lx_copy(r, e).wait_send()
        risk_ref[...] = jnp.where(real, risk_new, 0.0)

        for turn in range(2):
            rs_copy(0, 4, 1 - turn).wait_recv()
            rs_copy(1, 4, turn).wait_recv()
        for b in range(node_blks):
            pushed = (
                seg_ref[last_ref[b]]
                + segx_ref[chain_last[7 * node_blks + b]]
                + (ll_ref[3, b].astype(F32) + rr_ref[3, b].astype(F32))
            )
            dual = duals_ref[:, b * blk : (b + 1) * blk] + DUAL * (demand_ref[:, b * blk : (b + 1) * blk] - pushed)
            duals_ref[:, b * blk : (b + 1) * blk] = dual
            c0[b] = dual.astype(BF16)
        for direction in range(2):
            for step in range(1, 5):
                for h in range(2):
                    if step > 1 or h == direction:
                        rs_copy(direction, step, h).wait_send()
        for g in range(len(GROUPS)):
            for e in range(1, nx):
                f_copy(g, e).wait_send()

        @pl.when(r < ROUNDS - 1)
        def _():
            start_ring()

        return 0

    lax.fori_loop(0, ROUNDS, one_round, 0)
    excess_out[...] = excess_ref[:, 0:rows]
    risk_out[...] = risk_ref[:, 0:rows]
    level_out[...] = level_ref[:, 0:1]


def per_device(
    arc_flows,
    node_duals,
    demand,
    excess,
    risk_duals,
    threshold,
    arc_costs,
    local_blocks,
    head_blocks,
    local_index,
    head_index,
):
    blk = local_blocks.shape[-1]
    rows, arcs = arc_flows.shape
    arc_blks, touches = local_index.shape
    node_blks = node_duals.shape[1] // blk
    net = lax.axis_size("net")
    ns = lax.axis_size("scen")
    nx = net // NZ
    slots = NZ * SLOT
    smem = pl.BlockSpec(memory_space=pltpu.SMEM)
    vmem = pl.BlockSpec(memory_space=pltpu.VMEM)
    hbm = pl.BlockSpec(memory_space=pl.ANY)

    def ints(*shape):
        return jax.ShapeDtypeStruct(shape, jnp.int32)

    pos, slot_arc, want, prev, last = pl.pallas_call(
        functools.partial(table_kernel, nx, node_blks),
        out_shape=(ints(arc_blks), ints(nx * slots), ints(nx, 128), ints(arc_blks * touches), ints(node_blks)),
        in_specs=[smem, smem],
        out_specs=(smem,) * 5,
        scratch_shapes=[pltpu.SMEM((nx * NZ,), jnp.int32)],
        name="tables",
    )(head_index, local_index)

    def floats(*shape):
        return jax.ShapeDtypeStruct(shape, F32)

    def panel(*lead):
        return pltpu.VMEM((*lead, rows, blk), BF16)

    def wide(*lead):
        return pltpu.VMEM((*lead, rows, blk), F32)

    def row(*lead):
        return pltpu.VMEM((*lead, 1, blk), F32)

    dma = pltpu.SemaphoreType.DMA
    groups = len(GROUPS)
    scratch = (
        [pltpu.VMEM(local_blocks.shape, BF16), pltpu.VMEM(head_blocks.shape, BF16)]
        + [panel(node_blks)] * NZ
        + [
            pltpu.VMEM((nx, 128), jnp.int32),
            pltpu.SMEM((nx, 128), jnp.int32),
            pltpu.SMEM((NZ * nx * SLOT,), jnp.int32),
            pltpu.SMEM((NZ * node_blks,), jnp.int32),
            wide(arc_blks),
            panel(arc_blks),
            panel(arc_blks),
            wide(arc_blks * touches + 1),
            wide(NZ * nx * SLOT + 1),
            panel(nx, slots),
            panel(nx - 1, slots),
            panel(nx - 1, slots),
            panel(nx - 1, slots),
            panel(4, node_blks),
            panel(4, node_blks),
            panel(4, node_blks),
            panel(4, node_blks),
            row(),
            row(),
            row(),
            row(ROUNDS, nx),
            row(ROUNDS, NZ),
            row(ROUNDS, ns),
            dma((5,)),
        ]
        + [dma((nx - 1,))] * 2
        + [dma((16,))] * 2
        + [dma((groups * (nx - 1),))] * 4
        + [dma((16,))] * 2
        + [dma((ROUNDS * (nx - 1),))] * 2
        + [dma((ROUNDS * (NZ - 1),))] * 2
        + [dma((ROUNDS * (ns - 1),))] * 2
    )
    flows, duals, excess, risk, level = pl.pallas_call(
        functools.partial(main_kernel, nx, ns, float(rows * ns), float(arcs * net)),
        out_shape=(floats(rows, arcs), floats(*node_duals.shape), floats(1, rows), floats(1, rows), floats(1, 1)),
        in_specs=[hbm, hbm, vmem, vmem, vmem, vmem, vmem, hbm, hbm, smem, smem, smem, smem, vmem, smem, smem],
        out_specs=(vmem,) * 5,
        scratch_shapes=scratch,
        compiler_params=pltpu.CompilerParams(
            collective_id=0, has_side_effects=True, vmem_limit_bytes=48 * 1024 * 1024
        ),
        name="rounds",
    )(
        node_duals,
        arc_flows,
        demand,
        arc_costs.reshape(arc_blks, blk),
        excess.reshape(1, rows),
        risk_duals.reshape(1, rows),
        threshold.reshape(1, 1),
        local_blocks,
        head_blocks,
        local_index,
        pos,
        slot_arc,
        want,
        want,
        prev,
        last,
    )
    return flows, duals, excess.reshape(-1), risk.reshape(-1), level.reshape(-1)


def solution(mesh):
    placed = (
        P("scen", "net"),
        P("scen", "net"),
        P("scen", "net"),
        P("scen"),
        P("scen"),
        P(),
        P("net"),
        P("net", None, None, None),
        P("net", None, None),
        P("net", None),
        P("net"),
    )
    return jax.shard_map(
        per_device,
        mesh=mesh,
        in_specs=placed,
        out_specs=(P("scen", "net"), P("scen", "net"), P("scen"), P("scen"), P()),
        check_vma=False,
    )
```

```python
import functools

import jax
import jax.numpy as jnp
from jax import lax
from jax.experimental import pallas as pl
from jax.experimental.pallas import tpu as pltpu
from jax.sharding import PartitionSpec as P

ROUNDS = 3
NZ = 8
SLOT = 4
PRIMAL = 0.5
DUAL = 0.5
RISK = 1.0
TAIL = 2.0
MESH = pl.DeviceIdType.MESH
NT = (((1,), (1,)), ((), ()))
F32 = jnp.float32
BF16 = jnp.bfloat16
ORDER = (4, 3, 5, 2, 6, 1, 7, 0)
GROUPS = ((0, 1), (1, 2), (3, 2), (5, 2), (7, 1))
PARTS = 4
TURNS = ((0, 1, 2, 3), (2, 3, 0, 1))


def halves(n):
    return n.bit_length() - 1


def table_kernel(nx, node_blks, owner_vec, index_vec, own_rows, want_vec):
    touches, arc_blks = index_vec.shape
    blk = own_rows.shape[1]
    slots = NZ * SLOT
    me = lax.axis_index("net")
    x, z = me // NZ, me % NZ

    def count_of(mask, axis):
        return jnp.sum(jnp.where(mask, 1.0, 0.0), axis=axis, keepdims=True).astype(jnp.int32)

    def upright(row):
        n = row.shape[1]
        eye = lax.broadcasted_iota(jnp.int32, (n, n), 0) == lax.broadcasted_iota(jnp.int32, (n, n), 1)
        wide = jnp.broadcast_to(row.astype(F32), (n, n))
        return jnp.sum(jnp.where(eye, wide, 0.0), axis=1, keepdims=True).astype(jnp.int32)

    def highest(mask, value):
        return jnp.max(jnp.where(mask, value, 0.0), axis=0, keepdims=True)

    def place(heads):
        dev = lax.shift_right_logical(heads, halves(node_blks))
        e = (x - lax.shift_right_logical(dev, halves(NZ)) + nx) & (nx - 1)
        o = (z - (dev & (NZ - 1)) + NZ) & (NZ - 1)
        w = jnp.where(o >= 4, 2 * (o - 4), 7 - 2 * o)
        return dev, e * slots + w * SLOT

    square = (arc_blks, arc_blks)
    upper = lax.broadcasted_iota(jnp.int32, square, 0) < lax.broadcasted_iota(jnp.int32, square, 1)
    lower = lax.broadcasted_iota(jnp.int32, square, 0) > lax.broadcasted_iota(jnp.int32, square, 1)
    equal = lax.broadcasted_iota(jnp.int32, square, 0) == lax.broadcasted_iota(jnp.int32, square, 1)
    heads = owner_vec[...]
    heads_up = upright(heads)
    dev, base = place(heads)
    dev_up, base_up = place(heads_up)
    same = dev_up == dev
    pos = base + jnp.minimum(count_of(same & upper, 0), SLOT - 1)
    pos_up = base_up + jnp.minimum(count_of(same & lower, 1), SLOT - 1)
    flat = (arc_blks, nx * slots)
    filled = pos_up == lax.broadcasted_iota(jnp.int32, flat, 1)
    arc_number = lax.broadcasted_iota(jnp.int32, flat, 0).astype(F32)
    inside_up = (heads_up & (node_blks - 1)).astype(F32)
    arcs = highest(filled, arc_number)
    want = node_blks - highest(filled, node_blks - inside_up).astype(jnp.int32)
    want_vec[...] = want
    own_rows[...] = jnp.zeros_like(own_rows)
    own_rows[0:1, 0:arc_blks] = pos
    own_rows[1:2, :] = arcs.astype(jnp.int32)
    own_rows[7:8, :] = want
    step_up = lax.broadcasted_iota(jnp.int32, square, 0).astype(F32) * touches
    column = [upright(index_vec[k : k + 1, :]) for k in range(touches)]
    final = jnp.zeros((1, blk), F32)
    for k in range(touches):
        row = index_vec[k : k + 1, :]
        found = jnp.zeros((1, arc_blks), F32)
        for q in range(touches):
            before = (upper | equal) if q < k else upper
            found = jnp.maximum(found, highest((column[q] == row) & before, step_up + (q + 1)))
        own_rows[2 + k : 3 + k, 0:arc_blks] = found.astype(jnp.int32)
        wide = (arc_blks, blk)
        named = column[k] == lax.broadcasted_iota(jnp.int32, wide, 1)
        final = jnp.maximum(
            final, highest(named, lax.broadcasted_iota(jnp.int32, wide, 0).astype(F32) * touches + (k + 1))
        )
    own_rows[2 + touches : 3 + touches, :] = final.astype(jnp.int32)


def main_kernel(
    nx,
    ns,
    scen_total,
    arc_total,
    duals_hbm,
    flows_hbm,
    demand_hbm,
    cost_ref,
    excess_in,
    risk_in,
    level_in,
    local_hbm,
    head_hbm,
    index_ref,
    own_tab,
    want_vec,
    flows_out,
    duals_ref,
    excess_out,
    risk_out,
    level_out,
    local_ref,
    head_ref,
    flows_ref,
    demand_ref,
    c0, c1, c2, c3, c4, c5, c6, c7,
    ask_vec,
    ask_ref,
    ask_tab,
    pull_ref,
    panel_ref,
    seg_ref,
    segx_ref,
    hp_ref,
    own_ref,
    x_in,
    x_out,
    fx_in,
    fx_out,
    sl_ref,
    sr_ref,
    ll_ref,
    rr_ref,
    excess_ref,
    risk_ref,
    level_ref,
    lossx,
    lossz,
    scen_rows,
    load_sem,
    ask_send, ask_recv,
    ag_send, ag_recv,
    x_send, x_recv,
    f_send, f_recv,
    r_send, r_recv,
    lx_send, lx_recv,
    lz_send, lz_recv,
    sc_send, sc_recv,
):
    chunks = (c0, c1, c2, c3, c4, c5, c6, c7)
    touches, arc_blks = index_ref.shape
    rows = panel_ref.shape[1]
    blk = panel_ref.shape[2]
    node_blks = c0.shape[0]
    part_blks = node_blks // PARTS
    slots = NZ * SLOT
    me = lax.axis_index("net")
    scen = lax.axis_index("scen")
    x, z = me // NZ, me % NZ

    def x_peer(e):
        return {"net": lax.rem(x + e, nx) * NZ + z}

    def z_peer(d):
        return {"net": x * NZ + lax.rem(z + d, NZ)}

    def s_peer(d):
        return {"scen": lax.rem(scen + d, ns)}

    def remote(src, dst, send, recv, device):
        return pltpu.make_async_remote_copy(
            src_ref=src, dst_ref=dst, send_sem=send, recv_sem=recv, device_id=device, device_id_type=MESH
        )

    def columns(b):
        return pl.ds(pl.multiple_of(b * blk, blk), blk)

    def part(h):
        return pl.ds(h * part_blks, part_blks)

    def ag_copy(direction, step, h):
        n = step if direction == 0 else (NZ - step)
        src = chunks[step - 1] if direction == 0 else chunks[(NZ - step + 1) % NZ]
        i = (direction * 4 + step - 1) * PARTS + h
        return remote(
            src.at[part(h)], chunks[n].at[part(h)], ag_send.at[i], ag_recv.at[i], z_peer(1 if direction == 0 else NZ - 1)
        )

    def x_copy(g, e):
        first, count = GROUPS[g]
        i = g * (nx - 1) + e - 1
        return remote(
            x_out.at[pl.ds(e * slots + first * SLOT, count * SLOT)],
            x_in.at[pl.ds(e * slots + first * SLOT, count * SLOT)],
            x_send.at[i], x_recv.at[i], x_peer(e),
        )

    def f_copy(g, e):
        first, count = GROUPS[g]
        i = g * (nx - 1) + e - 1
        return remote(
            fx_out.at[pl.ds(e * slots + first * SLOT, count * SLOT)],
            fx_in.at[pl.ds(e * slots + first * SLOT, count * SLOT)],
            f_send.at[i], f_recv.at[i], x_peer(nx - e),
        )

    def rs_copy(direction, step, h):
        src = (sl_ref if direction == 0 else sr_ref).at[step - 1]
        dst = (ll_ref if direction == 0 else rr_ref).at[step - 1]
        i = (direction * 4 + step - 1) * PARTS + h
        return remote(
            src.at[part(h)], dst.at[part(h)], r_send.at[i], r_recv.at[i], z_peer(NZ - 1 if direction == 0 else 1)
        )

    def lx_copy(r, e):
        i = r * (nx - 1) + e - 1
        return remote(lossx.at[r, x], lossx.at[r, x], lx_send.at[i], lx_recv.at[i], x_peer(e))

    def lz_copy(r, d):
        i = r * (NZ - 1) + d - 1
        return remote(lossz.at[r, z], lossz.at[r, z], lz_send.at[i], lz_recv.at[i], z_peer(d))

    def sc_copy(r, d):
        i = r * (ns - 1) + d - 1
        return remote(scen_rows.at[r, scen], scen_rows.at[r, scen], sc_send.at[i], sc_recv.at[i], s_peer(d))

    def ask_copy(e):
        return remote(want_vec, ask_vec.at[pl.ds(e, 1)], ask_send.at[e - 1], ask_recv.at[e - 1], x_peer(nx - e))

    def start_ring():
        for turn in range(PARTS):
            ag_copy(0, 1, TURNS[0][turn]).start()
            ag_copy(1, 1, TURNS[1][turn]).start()

    loads = [
        pltpu.make_async_copy(src, dst, load_sem.at[i])
        for i, (src, dst) in enumerate(
            (
                (duals_hbm, duals_ref),
                (local_hbm, local_ref),
                (head_hbm, head_ref),
                (flows_hbm, flows_ref),
                (demand_hbm, demand_ref),
            )
        )
    ]
    for load in loads:
        load.start()
    barrier = pltpu.get_barrier_semaphore()
    peers = (
        [x_peer(e) for e in range(1, nx)] + [z_peer(d) for d in range(1, NZ)] + [s_peer(d) for d in range(1, ns)]
    )
    for peer in peers:
        pl.semaphore_signal(barrier, inc=1, device_id=peer, device_id_type=MESH)
    lane = lax.broadcasted_iota(jnp.int32, (rows, blk), 1)
    diagonal = lax.broadcasted_iota(jnp.int32, (rows, blk), 0) == lane
    real = lax.broadcasted_iota(jnp.int32, (1, blk), 1) < rows
    excess_ref[...] = jnp.zeros_like(excess_ref)
    risk_ref[...] = jnp.zeros_like(risk_ref)
    excess_ref[:, 0:rows] = excess_in[...]
    risk_ref[:, 0:rows] = risk_in[...]
    level_ref[...] = jnp.broadcast_to(level_in[...], level_ref.shape)
    seg_ref[0] = jnp.zeros((rows, blk), F32)
    segx_ref[0] = jnp.zeros((rows, blk), F32)

    loads[0].wait()
    for b in range(node_blks):
        c0[b] = duals_ref[:, b * blk : (b + 1) * blk].astype(BF16)
    pl.semaphore_wait(barrier, len(peers))
    for e in range(1, nx):
        ask_copy(e).start()
    start_ring()

    for e in range(1, nx):
        ask_copy(e).wait_recv()
    to_scalar = pltpu.make_async_copy(ask_vec, ask_ref, load_sem.at[5])
    to_scalar.start()
    to_scalar.wait()
    for e in range(1, nx):
        ask_copy(e).wait_send()

    def chain_tables(w, _):
        places = [q // SLOT * slots + w * SLOT + q % SLOT for q in range(nx * SLOT)]
        named = [
            own_tab[touches + 3, i] if q < SLOT else ask_ref[q // SLOT, i] for q, i in enumerate(places)
        ]
        for q, i in enumerate(places):
            found = jnp.int32(0)
            for p in range(q):
                found = jnp.where(named[p] == named[q], places[p] + 1, found)
            ask_tab[0, i] = jnp.minimum(named[q], node_blks - 1)
            ask_tab[1, i] = found
        for b in range(node_blks):
            found = jnp.int32(0)
            for q, i in enumerate(places):
                found = jnp.where(named[q] == b, i + 1, found)
            ask_tab[2, w * node_blks + b] = found
        return 0

    lax.fori_loop(0, NZ, chain_tables, 0)
    for load in loads[1:]:
        load.wait()

    def pull_local(first, count):
        def body(i, _):
            j = first + i
            total = jnp.zeros((rows, blk), F32)
            for k in range(touches):
                total += lax.dot_general(
                    c0[index_ref[k, j]], local_ref[j, k], NT, preferred_element_type=F32
                )
            pull_ref[j] = total
            return 0

        lax.fori_loop(0, count, body, 0, unroll=4)

    def push_local(first, count):
        def body(i, _):
            j = first + i
            v = panel_ref[j]
            for k in range(touches):
                term = jnp.dot(v, local_ref[j, k], preferred_element_type=F32)
                seg_ref[j * touches + k + 1] = term + seg_ref[own_tab[2 + k, j]]
            return 0

        lax.fori_loop(0, count, body, 0, unroll=4)

    def answer_group(g):
        first, count = GROUPS[g]
        for e in range(nx):
            for w in range(first, first + count):
                chunk = chunks[ORDER[w]]
                for s in range(SLOT):
                    i = e * slots + w * SLOT + s
                    (x_in if e == 0 else x_out)[i] = chunk[ask_tab[0, i]]
            if e > 0:
                x_copy(g, e).start()

    def pull_heads(g):
        first, count = GROUPS[g]

        def body(e, _):
            for s in range(count * SLOT):
                i = e * slots + first * SLOT + s
                hp_ref[i] = lax.dot_general(x_in[i], head_ref[own_tab[1, i]], NT, preferred_element_type=F32)
            return 0

        for e in range(1, nx):
            x_copy(g, e).wait_recv()
        lax.fori_loop(0, nx, body, 0)

    def push_heads(g):
        first, count = GROUPS[g]

        def term(e, s):
            j = own_tab[1, e * slots + first * SLOT + s]
            return jnp.dot(panel_ref[j], head_ref[j], preferred_element_type=F32)

        def body(e, _):
            for s in range(count * SLOT):
                fx_out[e * slots + first * SLOT + s] = term(e, s).astype(BF16)
            return 0

        lax.fori_loop(1, nx, body, 0)
        for e in range(1, nx):
            f_copy(g, e).start()
        for s in range(count * SLOT):
            own_ref[first * SLOT + s] = term(0, s)

    def collect(w):
        for q in range(nx * SLOT):
            e = q // SLOT
            i = w * SLOT + q % SLOT
            n = e * slots + i
            value = own_ref[i] if e == 0 else fx_in[n].astype(F32)
            segx_ref[n + 1] = value + segx_ref[ask_tab[1, n]]

    def send_sum(direction, step, h, with_arrived):
        w = ORDER.index(5 - step if direction == 0 else 3 + step)
        dst = sl_ref if direction == 0 else sr_ref
        arrived = ll_ref if direction == 0 else rr_ref
        if with_arrived:
            rs_copy(direction, step - 1, h).wait_recv()
        for b in range(h * part_blks, (h + 1) * part_blks):
            value = segx_ref[ask_tab[2, w * node_blks + b]]
            if with_arrived:
                value = value + arrived[step - 2, b].astype(F32)
            dst[step - 1, b] = value.astype(BF16)
        rs_copy(direction, step, h).start()

    def one_round(r, _):
        scen_rows[r, scen] = risk_ref[...]
        for d in range(1, ns):
            sc_copy(r, d).start()
        piece = arc_blks // 16
        answer_group(4)
        pull_local(0, 4 * piece)
        done = 4
        for step in range(1, 4):
            for turn in range(PARTS):
                for direction in range(2):
                    h = TURNS[direction][turn]
                    ag_copy(direction, step, h).wait_recv()
                    if step < 3 or turn < PARTS // 2:
                        ag_copy(direction, step + 1, h).start()
                if turn == PARTS - 1:
                    answer_group(4 - step)
                pull_local(done * piece, piece)
                done += 1
            if step > 1:
                pull_heads(6 - step)
        for turn in range(PARTS // 2):
            for direction in range(2):
                ag_copy(direction, 4, TURNS[direction][turn]).wait_recv()
        answer_group(0)
        risk_wide = jnp.broadcast_to(
            jnp.sum(jnp.where(diagonal, jnp.broadcast_to(risk_ref[...], (rows, blk)), 0.0), axis=1, keepdims=True),
            (rows, blk),
        )
        for g in (2, 1, 0):
            pull_heads(g)

        def move(i, loss):
            js = [i * 4 + u for u in range(4)]
            pulled = [pull_ref[j] + hp_ref[own_tab[0, j]] for j in js]
            costs = [jnp.broadcast_to(cost_ref[pl.ds(j, 1), :], (rows, blk)) for j in js]
            now = [flows_ref[:, columns(j)] for j in js]
            new = [jnp.maximum(n - PRIMAL * (risk_wide * c - p), 0.0) for n, c, p in zip(now, costs, pulled)]
            bars = [2.0 * v - n for v, n in zip(new, now)]
            for j, v, bar in zip(js, new, bars):
                flows_ref[:, columns(j)] = v
                panel_ref[j] = bar.astype(BF16)
            for c, bar in zip(costs, bars):
                loss = loss + c * bar
            return loss

        loss = lax.fori_loop(0, arc_blks // 4, move, jnp.zeros((rows, blk), F32))
        keep = pltpu.make_async_copy(flows_ref, flows_out, load_sem.at[7])

        @pl.when(r == ROUNDS - 1)
        def _():
            keep.start()

        for g in range(len(GROUPS)):
            push_heads(g)
        wide = jnp.broadcast_to(jnp.sum(loss, axis=1, keepdims=True), (rows, blk))
        lossx[r, x] = jnp.sum(jnp.where(diagonal, wide, 0.0), axis=0, keepdims=True)
        for e in range(1, nx):
            lx_copy(r, e).start()
        for direction in range(2):
            for step in range(1, 5):
                for turn in range(PARTS):
                    if step < 4 or turn < PARTS // 2:
                        ag_copy(direction, step, TURNS[direction][turn]).wait_send()
        for g in range(len(GROUPS)):
            for e in range(1, nx):
                x_copy(g, e).wait_send()
        push_local(0, 4 * piece)

        for e in range(1, nx):
            f_copy(0, e).wait_recv()
        collect(0)
        for turn in range(PARTS // 2):
            for direction in range(2):
                send_sum(direction, 1, TURNS[direction][turn], False)
        for e in range(1, nx):
            lx_copy(r, e).wait_recv()
        total = lossx[r, 0]
        for i in range(1, nx):
            total = total + lossx[r, i]
        lossz[r, z] = total
        for d in range(1, NZ):
            lz_copy(r, d).start()
        done = 4
        for step in range(2, 5):
            for e in range(1, nx):
                f_copy(step - 1, e).wait_recv()
            collect(2 * step - 3)
            collect(2 * step - 2)
            for turn in range(PARTS):
                for direction in range(2):
                    send_sum(direction, step, TURNS[1 - direction][turn], step > 2 or turn >= PARTS // 2)
                push_local(done * piece, piece)
                done += 1
        for e in range(1, nx):
            f_copy(4, e).wait_recv()
        collect(7)

        for d in range(1, NZ):
            lz_copy(r, d).wait_recv()
        losses = lossz[r, 0]
        for i in range(1, NZ):
            losses = losses + lossz[r, i]
        losses = losses / arc_total
        for d in range(1, ns):
            sc_copy(r, d).wait_recv()
        risk_sum = scen_rows[r, 0]
        for i in range(1, ns):
            risk_sum = risk_sum + scen_rows[r, i]
        mean = jnp.broadcast_to(jnp.sum(risk_sum, axis=1, keepdims=True), (1, blk)) / scen_total
        risk = risk_ref[...]
        excess = excess_ref[...]
        level = level_ref[...]
        excess_new = jnp.maximum(excess - PRIMAL * (TAIL - risk), 0.0)
        level_new = level - PRIMAL * (1.0 - mean)
        excess_bar = 2.0 * excess_new - excess
        level_bar = 2.0 * level_new - level
        risk_new = jnp.maximum(risk + RISK * (losses - excess_bar - level_bar), 0.0)
        excess_ref[...] = excess_new
        level_ref[...] = level_new
        for d in range(1, ns):
            sc_copy(r, d).wait_send()
        for d in range(1, NZ):
            lz_copy(r, d).wait_send()
        for e in range(1, nx):
            lx_copy(r, e).wait_send()
        risk_ref[...] = jnp.where(real, risk_new, 0.0)

        for turn in range(PARTS):
            for direction in range(2):
                rs_copy(direction, 4, TURNS[1 - direction][turn]).wait_recv()
        for b in range(node_blks):
            pushed = (
                seg_ref[own_tab[2 + touches, b]]
                + segx_ref[ask_tab[2, 7 * node_blks + b]]
                + (ll_ref[3, b].astype(F32) + rr_ref[3, b].astype(F32))
            )
            dual = duals_ref[:, b * blk : (b + 1) * blk] + DUAL * (demand_ref[:, b * blk : (b + 1) * blk] - pushed)
            duals_ref[:, b * blk : (b + 1) * blk] = dual
            c0[b] = dual.astype(BF16)
        for direction in range(2):
            for step in range(1, 5):
                for turn in range(PARTS):
                    if step > 1 or turn < PARTS // 2:
                        rs_copy(direction, step, TURNS[direction][turn]).wait_send()
        for g in range(len(GROUPS)):
            for e in range(1, nx):
                f_copy(g, e).wait_send()

        @pl.when(r < ROUNDS - 1)
        def _():
            start_ring()

        return 0

    lax.fori_loop(0, ROUNDS, one_round, 0)
    pltpu.make_async_copy(flows_ref, flows_out, load_sem.at[7]).wait()
    excess_out[...] = excess_ref[:, 0:rows]
    risk_out[...] = risk_ref[:, 0:rows]
    level_out[...] = level_ref[:, 0:1]


def per_device(
    arc_flows,
    node_duals,
    demand,
    excess,
    risk_duals,
    threshold,
    arc_costs,
    local_blocks,
    head_blocks,
    local_index,
    head_index,
):
    blk = local_blocks.shape[-1]
    rows, arcs = arc_flows.shape
    arc_blks, touches = local_index.shape
    node_blks = node_duals.shape[1] // blk
    net = lax.axis_size("net")
    ns = lax.axis_size("scen")
    nx = net // NZ
    slots = NZ * SLOT
    smem = pl.BlockSpec(memory_space=pltpu.SMEM)
    vmem = pl.BlockSpec(memory_space=pltpu.VMEM)
    hbm = pl.BlockSpec(memory_space=pl.ANY)

    def floats(*shape):
        return jax.ShapeDtypeStruct(shape, F32)

    def panel(*lead):
        return pltpu.VMEM((*lead, rows, blk), BF16)

    def wide(*lead):
        return pltpu.VMEM((*lead, rows, blk), F32)

    def row(*lead):
        return pltpu.VMEM((*lead, 1, blk), F32)

    dma = pltpu.SemaphoreType.DMA
    groups = len(GROUPS)
    scratch = (
        [
            pltpu.VMEM(local_blocks.shape, BF16),
            pltpu.VMEM(head_blocks.shape, BF16),
            pltpu.VMEM(arc_flows.shape, F32),
            pltpu.VMEM(demand.shape, F32),
        ]
        + [panel(node_blks)] * NZ
        + [
            pltpu.VMEM((nx, nx * slots), jnp.int32),
            pltpu.SMEM((nx, nx * slots), jnp.int32),
            pltpu.SMEM((4, 128), jnp.int32),
            wide(arc_blks),
            panel(arc_blks),
            wide(arc_blks * touches + 1),
            wide(nx * slots + 1),
            wide(nx * slots),
            wide(slots),
            panel(nx * slots),
            panel(nx * slots),
            panel(nx * slots),
            panel(nx * slots),
            panel(4, node_blks),
            panel(4, node_blks),
            panel(4, node_blks),
            panel(4, node_blks),
            row(),
            row(),
            row(),
            row(ROUNDS, nx),
            row(ROUNDS, NZ),
            row(ROUNDS, ns),
            dma((8,)),
        ]
        + [dma((nx - 1,))] * 2
        + [dma((8 * PARTS,))] * 2
        + [dma((groups * (nx - 1),))] * 4
        + [dma((8 * PARTS,))] * 2
        + [dma((ROUNDS * (nx - 1),))] * 2
        + [dma((ROUNDS * (NZ - 1),))] * 2
        + [dma((ROUNDS * (ns - 1),))] * 2
    )
    own, want = pl.pallas_call(
        functools.partial(table_kernel, nx, node_blks),
        out_shape=(
            jax.ShapeDtypeStruct((8, blk), jnp.int32),
            jax.ShapeDtypeStruct((1, nx * slots), jnp.int32),
        ),
        in_specs=[vmem, vmem],
        out_specs=(vmem, vmem),
        name="tables",
    )(head_index.reshape(1, arc_blks), local_index.T)
    flows, duals, excess, risk, level = pl.pallas_call(
        functools.partial(main_kernel, nx, ns, float(rows * ns), float(arcs * net)),
        out_shape=(floats(rows, arcs), floats(*node_duals.shape), floats(1, rows), floats(1, rows), floats(1, 1)),
        in_specs=[hbm, hbm, hbm, vmem, vmem, vmem, vmem, hbm, hbm, smem, smem, vmem],
        out_specs=(hbm, vmem, vmem, vmem, vmem),
        scratch_shapes=scratch,
        compiler_params=pltpu.CompilerParams(
            collective_id=0, has_side_effects=True, vmem_limit_bytes=67043328
        ),
        name="rounds",
    )(
        node_duals,
        arc_flows,
        demand,
        arc_costs.reshape(arc_blks, blk),
        excess.reshape(1, rows),
        risk_duals.reshape(1, rows),
        threshold.reshape(1, 1),
        local_blocks,
        head_blocks,
        local_index.T,
        own,
        want,
    )
    return flows, duals, excess.reshape(-1), risk.reshape(-1), level.reshape(-1)


def solution(mesh):
    placed = (
        P("scen", "net"),
        P("scen", "net"),
        P("scen", "net"),
        P("scen"),
        P("scen"),
        P(),
        P("net"),
        P("net", None, None, None),
        P("net", None, None),
        P("net", None),
        P("net"),
    )
    return jax.shard_map(
        per_device,
        mesh=mesh,
        in_specs=placed,
        out_specs=(P("scen", "net"), P("scen", "net"), P("scen"), P("scen"), P()),
        check_vma=False,
    )
```

```python
import functools

import jax
import jax.numpy as jnp
from jax import lax
from jax.experimental import pallas as pl
from jax.experimental.pallas import tpu as pltpu
from jax.sharding import PartitionSpec as P

ROUNDS = 3
NZ = 8
SLOT = 4
PRIMAL = 0.5
DUAL = 0.5
RISK = 1.0
TAIL = 2.0
MESH = pl.DeviceIdType.MESH
NT = (((1,), (1,)), ((), ()))
F32 = jnp.float32
BF16 = jnp.bfloat16
ORDER = (4, 3, 5, 2, 6, 1, 7, 0)
GROUPS = ((0, 1), (1, 2), (3, 2), (5, 2), (7, 1))
PARTS = 4
TURNS = ((0, 1, 2, 3), (2, 3, 0, 1))


def halves(n):
    return n.bit_length() - 1


def table_kernel(nx, node_blks, owner_vec, index_vec, own_rows, want_vec):
    touches, arc_blks = index_vec.shape
    blk = own_rows.shape[1]
    slots = NZ * SLOT
    me = lax.axis_index("net")
    x, z = me // NZ, me % NZ

    def count_of(mask, axis):
        return jnp.sum(jnp.where(mask, 1.0, 0.0), axis=axis, keepdims=True).astype(jnp.int32)

    def upright(row):
        n = row.shape[1]
        eye = lax.broadcasted_iota(jnp.int32, (n, n), 0) == lax.broadcasted_iota(jnp.int32, (n, n), 1)
        wide = jnp.broadcast_to(row.astype(F32), (n, n))
        return jnp.sum(jnp.where(eye, wide, 0.0), axis=1, keepdims=True).astype(jnp.int32)

    def highest(mask, value):
        return jnp.max(jnp.where(mask, value, 0.0), axis=0, keepdims=True)

    def place(heads):
        dev = lax.shift_right_logical(heads, halves(node_blks))
        e = (x - lax.shift_right_logical(dev, halves(NZ)) + nx) & (nx - 1)
        o = (z - (dev & (NZ - 1)) + NZ) & (NZ - 1)
        w = jnp.where(o >= 4, 2 * (o - 4), 7 - 2 * o)
        return dev, e * slots + w * SLOT

    square = (arc_blks, arc_blks)
    upper = lax.broadcasted_iota(jnp.int32, square, 0) < lax.broadcasted_iota(jnp.int32, square, 1)
    lower = lax.broadcasted_iota(jnp.int32, square, 0) > lax.broadcasted_iota(jnp.int32, square, 1)
    equal = lax.broadcasted_iota(jnp.int32, square, 0) == lax.broadcasted_iota(jnp.int32, square, 1)
    heads = owner_vec[...]
    heads_up = upright(heads)
    dev, base = place(heads)
    dev_up, base_up = place(heads_up)
    same = dev_up == dev
    pos = base + jnp.minimum(count_of(same & upper, 0), SLOT - 1)
    pos_up = base_up + jnp.minimum(count_of(same & lower, 1), SLOT - 1)
    flat = (arc_blks, nx * slots)
    filled = pos_up == lax.broadcasted_iota(jnp.int32, flat, 1)
    arc_number = lax.broadcasted_iota(jnp.int32, flat, 0).astype(F32)
    inside_up = (heads_up & (node_blks - 1)).astype(F32)
    arcs = highest(filled, arc_number)
    want = node_blks - highest(filled, node_blks - inside_up).astype(jnp.int32)
    want_vec[...] = want
    own_rows[...] = jnp.zeros_like(own_rows)
    own_rows[0:1, 0:arc_blks] = pos
    own_rows[1:2, :] = arcs.astype(jnp.int32)
    own_rows[7:8, :] = want
    step_up = lax.broadcasted_iota(jnp.int32, square, 0).astype(F32) * touches
    column = [upright(index_vec[k : k + 1, :]) for k in range(touches)]
    final = jnp.zeros((1, blk), F32)
    for k in range(touches):
        row = index_vec[k : k + 1, :]
        found = jnp.zeros((1, arc_blks), F32)
        for q in range(touches):
            before = (upper | equal) if q < k else upper
            found = jnp.maximum(found, highest((column[q] == row) & before, step_up + (q + 1)))
        own_rows[2 + k : 3 + k, 0:arc_blks] = found.astype(jnp.int32)
        wide = (arc_blks, blk)
        named = column[k] == lax.broadcasted_iota(jnp.int32, wide, 1)
        final = jnp.maximum(
            final, highest(named, lax.broadcasted_iota(jnp.int32, wide, 0).astype(F32) * touches + (k + 1))
        )
    own_rows[2 + touches : 3 + touches, :] = final.astype(jnp.int32)


def main_kernel(
    nx,
    ns,
    scen_total,
    arc_total,
    duals_hbm,
    flows_hbm,
    demand_hbm,
    cost_ref,
    excess_in,
    risk_in,
    level_in,
    local_hbm,
    head_hbm,
    index_ref,
    own_tab,
    want_vec,
    flows_out,
    duals_ref,
    excess_out,
    risk_out,
    level_out,
    local_ref,
    head_ref,
    flows_ref,
    demand_ref,
    c0, c1, c2, c3, c4, c5, c6, c7,
    ask_vec,
    ask_ref,
    ask_tab,
    pull_ref,
    panel_ref,
    seg_ref,
    segx_ref,
    hp_ref,
    own_ref,
    x_in,
    x_out,
    fx_in,
    fx_out,
    sl_ref,
    sr_ref,
    ll_ref,
    rr_ref,
    excess_ref,
    risk_ref,
    level_ref,
    lossx,
    lossz,
    scen_rows,
    load_sem,
    ask_send, ask_recv,
    ag_send, ag_recv,
    x_send, x_recv,
    f_send, f_recv,
    r_send, r_recv,
    lx_send, lx_recv,
    lz_send, lz_recv,
    sc_send, sc_recv,
):
    chunks = (c0, c1, c2, c3, c4, c5, c6, c7)
    touches, arc_blks = index_ref.shape
    rows = panel_ref.shape[1]
    blk = panel_ref.shape[2]
    node_blks = c0.shape[0]
    part_blks = node_blks // PARTS
    slots = NZ * SLOT
    me = lax.axis_index("net")
    scen = lax.axis_index("scen")
    x, z = me // NZ, me % NZ

    def x_peer(e):
        return {"net": lax.rem(x + e, nx) * NZ + z}

    def z_peer(d):
        return {"net": x * NZ + lax.rem(z + d, NZ)}

    def s_peer(d):
        return {"scen": lax.rem(scen + d, ns)}

    def remote(src, dst, send, recv, device):
        return pltpu.make_async_remote_copy(
            src_ref=src, dst_ref=dst, send_sem=send, recv_sem=recv, device_id=device, device_id_type=MESH
        )

    def columns(b):
        return pl.ds(pl.multiple_of(b * blk, blk), blk)

    def part(h):
        return pl.ds(h * part_blks, part_blks)

    def ag_copy(direction, step, h):
        n = step if direction == 0 else (NZ - step)
        src = chunks[step - 1] if direction == 0 else chunks[(NZ - step + 1) % NZ]
        i = (direction * 4 + step - 1) * PARTS + h
        return remote(
            src.at[part(h)], chunks[n].at[part(h)], ag_send.at[i], ag_recv.at[i], z_peer(1 if direction == 0 else NZ - 1)
        )

    def x_copy(g, e):
        first, count = GROUPS[g]
        i = g * (nx - 1) + e - 1
        return remote(
            x_out.at[pl.ds(e * slots + first * SLOT, count * SLOT)],
            x_in.at[pl.ds(e * slots + first * SLOT, count * SLOT)],
            x_send.at[i], x_recv.at[i], x_peer(e),
        )

    def f_copy(g, e):
        first, count = GROUPS[g]
        i = g * (nx - 1) + e - 1
        return remote(
            fx_out.at[pl.ds(e * slots + first * SLOT, count * SLOT)],
            fx_in.at[pl.ds(e * slots + first * SLOT, count * SLOT)],
            f_send.at[i], f_recv.at[i], x_peer(nx - e),
        )

    def rs_copy(direction, step, h):
        src = (sl_ref if direction == 0 else sr_ref).at[step - 1]
        dst = (ll_ref if direction == 0 else rr_ref).at[step - 1]
        i = (direction * 4 + step - 1) * PARTS + h
        return remote(
            src.at[part(h)], dst.at[part(h)], r_send.at[i], r_recv.at[i], z_peer(NZ - 1 if direction == 0 else 1)
        )

    def lx_copy(r, e):
        i = r * (nx - 1) + e - 1
        return remote(lossx.at[r, x], lossx.at[r, x], lx_send.at[i], lx_recv.at[i], x_peer(e))

    def lz_copy(r, d):
        i = r * (NZ - 1) + d - 1
        return remote(lossz.at[r, z], lossz.at[r, z], lz_send.at[i], lz_recv.at[i], z_peer(d))

    def sc_copy(r, d):
        i = r * (ns - 1) + d - 1
        return remote(scen_rows.at[r, scen], scen_rows.at[r, scen], sc_send.at[i], sc_recv.at[i], s_peer(d))

    def ask_copy(e):
        return remote(want_vec, ask_vec.at[pl.ds(e, 1)], ask_send.at[e - 1], ask_recv.at[e - 1], x_peer(nx - e))

    def start_ring():
        for turn in range(PARTS):
            ag_copy(0, 1, TURNS[0][turn]).start()
            ag_copy(1, 1, TURNS[1][turn]).start()

    loads = [
        pltpu.make_async_copy(src, dst, load_sem.at[i])
        for i, (src, dst) in enumerate(
            (
                (duals_hbm, duals_ref),
                (local_hbm, local_ref),
                (head_hbm, head_ref),
                (flows_hbm, flows_ref),
                (demand_hbm, demand_ref),
            )
        )
    ]
    for load in loads:
        load.start()
    barrier = pltpu.get_barrier_semaphore()
    peers = (
        [x_peer(e) for e in range(1, nx)] + [z_peer(d) for d in range(1, NZ)] + [s_peer(d) for d in range(1, ns)]
    )
    for peer in peers:
        pl.semaphore_signal(barrier, inc=1, device_id=peer, device_id_type=MESH)
    lane = lax.broadcasted_iota(jnp.int32, (rows, blk), 1)
    diagonal = lax.broadcasted_iota(jnp.int32, (rows, blk), 0) == lane
    real = lax.broadcasted_iota(jnp.int32, (1, blk), 1) < rows
    excess_ref[...] = jnp.zeros_like(excess_ref)
    risk_ref[...] = jnp.zeros_like(risk_ref)
    excess_ref[:, 0:rows] = excess_in[...]
    risk_ref[:, 0:rows] = risk_in[...]
    level_ref[...] = jnp.broadcast_to(level_in[...], level_ref.shape)
    seg_ref[0] = jnp.zeros((rows, blk), F32)
    segx_ref[0] = jnp.zeros((rows, blk), F32)

    loads[0].wait()
    for b in range(node_blks):
        c0[b] = duals_ref[:, b * blk : (b + 1) * blk].astype(BF16)
    pl.semaphore_wait(barrier, len(peers))
    for e in range(1, nx):
        ask_copy(e).start()
    start_ring()

    for e in range(1, nx):
        ask_copy(e).wait_recv()
    to_scalar = pltpu.make_async_copy(ask_vec, ask_ref, load_sem.at[5])
    to_scalar.start()
    to_scalar.wait()
    for e in range(1, nx):
        ask_copy(e).wait_send()

    def chain_tables(w, _):
        places = [q // SLOT * slots + w * SLOT + q % SLOT for q in range(nx * SLOT)]
        named = [
            own_tab[touches + 3, i] if q < SLOT else ask_ref[q // SLOT, i] for q, i in enumerate(places)
        ]
        for q, i in enumerate(places):
            found = jnp.int32(0)
            for p in range(q):
                found = jnp.where(named[p] == named[q], places[p] + 1, found)
            ask_tab[0, i] = found
        for b in range(node_blks):
            found = jnp.int32(0)
            for q, i in enumerate(places):
                found = jnp.where(named[q] == b, i + 1, found)
            ask_tab[1, w * node_blks + b] = found
        return 0

    for load in loads[1:]:
        load.wait()

    def pull_local(first, count):
        def body(i, _):
            j = first + i
            total = jnp.zeros((rows, blk), F32)
            for k in range(touches):
                total += lax.dot_general(
                    c0[index_ref[k, j]], local_ref[j, k], NT, preferred_element_type=F32
                )
            pull_ref[j] = total
            return 0

        lax.fori_loop(0, count, body, 0, unroll=4)

    def push_local(first, count):
        def body(i, _):
            j = first + i
            v = panel_ref[j]
            for k in range(touches):
                term = jnp.dot(v, local_ref[j, k], preferred_element_type=F32)
                seg_ref[j * touches + k + 1] = term + seg_ref[own_tab[2 + k, j]]
            return 0

        lax.fori_loop(0, count, body, 0, unroll=4)

    def answer_group(g):
        first, count = GROUPS[g]
        for e in range(nx):
            for w in range(first, first + count):
                chunk = chunks[ORDER[w]]
                for s in range(SLOT):
                    i = e * slots + w * SLOT + s
                    named = own_tab[touches + 3, i] if e == 0 else ask_ref[e, i]
                    (x_in if e == 0 else x_out)[i] = chunk[jnp.minimum(named, node_blks - 1)]
            if e > 0:
                x_copy(g, e).start()

    def pull_heads(g):
        first, count = GROUPS[g]

        def body(e, _):
            for s in range(count * SLOT):
                i = e * slots + first * SLOT + s
                hp_ref[i] = lax.dot_general(x_in[i], head_ref[own_tab[1, i]], NT, preferred_element_type=F32)
            return 0

        for e in range(1, nx):
            x_copy(g, e).wait_recv()
        lax.fori_loop(0, nx, body, 0)

    def push_heads(g):
        first, count = GROUPS[g]

        def term(e, s):
            j = own_tab[1, e * slots + first * SLOT + s]
            return jnp.dot(panel_ref[j], head_ref[j], preferred_element_type=F32)

        def body(e, _):
            for s in range(count * SLOT):
                fx_out[e * slots + first * SLOT + s] = term(e, s).astype(BF16)
            return 0

        lax.fori_loop(1, nx, body, 0)
        for e in range(1, nx):
            f_copy(g, e).start()
        for s in range(count * SLOT):
            own_ref[first * SLOT + s] = term(0, s)

    def collect(w):
        for q in range(nx * SLOT):
            e = q // SLOT
            i = w * SLOT + q % SLOT
            n = e * slots + i
            value = own_ref[i] if e == 0 else fx_in[n].astype(F32)
            segx_ref[n + 1] = value + segx_ref[ask_tab[0, n]]

    def send_sum(direction, step, h, with_arrived):
        w = ORDER.index(5 - step if direction == 0 else 3 + step)
        dst = sl_ref if direction == 0 else sr_ref
        arrived = ll_ref if direction == 0 else rr_ref
        if with_arrived:
            rs_copy(direction, step - 1, h).wait_recv()
        for b in range(h * part_blks, (h + 1) * part_blks):
            value = segx_ref[ask_tab[1, w * node_blks + b]]
            if with_arrived:
                value = value + arrived[step - 2, b].astype(F32)
            dst[step - 1, b] = value.astype(BF16)
        rs_copy(direction, step, h).start()

    def one_round(r, _):
        scen_rows[r, scen] = risk_ref[...]
        for d in range(1, ns):
            sc_copy(r, d).start()
        piece = arc_blks // 16
        answer_group(4)
        pull_local(0, 4 * piece)
        done = 4
        for step in range(1, 4):
            for turn in range(PARTS):
                for direction in range(2):
                    h = TURNS[direction][turn]
                    ag_copy(direction, step, h).wait_recv()
                    if step < 3 or turn < PARTS // 2:
                        ag_copy(direction, step + 1, h).start()
                if turn == PARTS - 1:
                    answer_group(4 - step)
                pull_local(done * piece, piece)
                done += 1
            if step > 1:
                pull_heads(6 - step)
        for turn in range(PARTS // 2):
            for direction in range(2):
                ag_copy(direction, 4, TURNS[direction][turn]).wait_recv()
        answer_group(0)

        @pl.when(r == 0)
        def _():
            lax.fori_loop(0, NZ, chain_tables, 0)

        risk_wide = jnp.broadcast_to(
            jnp.sum(jnp.where(diagonal, jnp.broadcast_to(risk_ref[...], (rows, blk)), 0.0), axis=1, keepdims=True),
            (rows, blk),
        )
        for g in (2, 1, 0):
            pull_heads(g)

        def move(i, loss):
            js = [i * 4 + u for u in range(4)]
            pulled = [pull_ref[j] + hp_ref[own_tab[0, j]] for j in js]
            costs = [jnp.broadcast_to(cost_ref[pl.ds(j, 1), :], (rows, blk)) for j in js]
            now = [flows_ref[:, columns(j)] for j in js]
            new = [jnp.maximum(n - PRIMAL * (risk_wide * c - p), 0.0) for n, c, p in zip(now, costs, pulled)]
            bars = [2.0 * v - n for v, n in zip(new, now)]
            for j, v, bar in zip(js, new, bars):
                flows_ref[:, columns(j)] = v
                panel_ref[j] = bar.astype(BF16)
            for c, bar in zip(costs, bars):
                loss = loss + c * bar
            return loss

        loss = lax.fori_loop(0, arc_blks // 4, move, jnp.zeros((rows, blk), F32))
        keep = pltpu.make_async_copy(flows_ref, flows_out, load_sem.at[7])

        @pl.when(r == ROUNDS - 1)
        def _():
            keep.start()

        for g in range(len(GROUPS)):
            push_heads(g)
        wide = jnp.broadcast_to(jnp.sum(loss, axis=1, keepdims=True), (rows, blk))
        lossx[r, x] = jnp.sum(jnp.where(diagonal, wide, 0.0), axis=0, keepdims=True)
        for e in range(1, nx):
            lx_copy(r, e).start()
        for direction in range(2):
            for step in range(1, 5):
                for turn in range(PARTS):
                    if step < 4 or turn < PARTS // 2:
                        ag_copy(direction, step, TURNS[direction][turn]).wait_send()
        for g in range(len(GROUPS)):
            for e in range(1, nx):
                x_copy(g, e).wait_send()
        push_local(0, 4 * piece)

        for e in range(1, nx):
            f_copy(0, e).wait_recv()
        collect(0)
        for turn in range(PARTS // 2):
            for direction in range(2):
                send_sum(direction, 1, TURNS[direction][turn], False)
        for e in range(1, nx):
            lx_copy(r, e).wait_recv()
        total = lossx[r, 0]
        for i in range(1, nx):
            total = total + lossx[r, i]
        lossz[r, z] = total
        for d in range(1, NZ):
            lz_copy(r, d).start()
        done = 4
        for step in range(2, 5):
            for e in range(1, nx):
                f_copy(step - 1, e).wait_recv()
            collect(2 * step - 3)
            collect(2 * step - 2)
            for turn in range(PARTS):
                for direction in range(2):
                    send_sum(direction, step, TURNS[1 - direction][turn], step > 2 or turn >= PARTS // 2)
                push_local(done * piece, piece)
                done += 1
        for e in range(1, nx):
            f_copy(4, e).wait_recv()
        collect(7)

        for turn in range(PARTS):
            for direction in range(2):
                rs_copy(direction, 4, TURNS[1 - direction][turn]).wait_recv()
        for b in range(node_blks):
            pushed = (
                seg_ref[own_tab[2 + touches, b]]
                + segx_ref[ask_tab[1, 7 * node_blks + b]]
                + (ll_ref[3, b].astype(F32) + rr_ref[3, b].astype(F32))
            )
            dual = duals_ref[:, b * blk : (b + 1) * blk] + DUAL * (demand_ref[:, b * blk : (b + 1) * blk] - pushed)
            duals_ref[:, b * blk : (b + 1) * blk] = dual
            c0[b] = dual.astype(BF16)
        @pl.when(r < ROUNDS - 1)
        def _():
            start_ring()

        for direction in range(2):
            for step in range(1, 5):
                for turn in range(PARTS):
                    if step > 1 or turn < PARTS // 2:
                        rs_copy(direction, step, TURNS[direction][turn]).wait_send()
        for g in range(len(GROUPS)):
            for e in range(1, nx):
                f_copy(g, e).wait_send()

        for d in range(1, NZ):
            lz_copy(r, d).wait_recv()
        losses = lossz[r, 0]
        for i in range(1, NZ):
            losses = losses + lossz[r, i]
        losses = losses / arc_total
        for d in range(1, ns):
            sc_copy(r, d).wait_recv()
        risk_sum = scen_rows[r, 0]
        for i in range(1, ns):
            risk_sum = risk_sum + scen_rows[r, i]
        mean = jnp.broadcast_to(jnp.sum(risk_sum, axis=1, keepdims=True), (1, blk)) / scen_total
        risk = risk_ref[...]
        excess = excess_ref[...]
        level = level_ref[...]
        excess_new = jnp.maximum(excess - PRIMAL * (TAIL - risk), 0.0)
        level_new = level - PRIMAL * (1.0 - mean)
        excess_bar = 2.0 * excess_new - excess
        level_bar = 2.0 * level_new - level
        risk_new = jnp.maximum(risk + RISK * (losses - excess_bar - level_bar), 0.0)
        excess_ref[...] = excess_new
        level_ref[...] = level_new
        for d in range(1, ns):
            sc_copy(r, d).wait_send()
        for d in range(1, NZ):
            lz_copy(r, d).wait_send()
        for e in range(1, nx):
            lx_copy(r, e).wait_send()
        risk_ref[...] = jnp.where(real, risk_new, 0.0)
        return 0

    lax.fori_loop(0, ROUNDS, one_round, 0)
    pltpu.make_async_copy(flows_ref, flows_out, load_sem.at[7]).wait()
    excess_out[...] = excess_ref[:, 0:rows]
    risk_out[...] = risk_ref[:, 0:rows]
    level_out[...] = level_ref[:, 0:1]


def finish_kernel(*refs):
    for src, dst in zip(refs[:5], refs[5:]):
        dst[...] = src[...]


def per_device(
    arc_flows,
    node_duals,
    demand,
    excess,
    risk_duals,
    threshold,
    arc_costs,
    local_blocks,
    head_blocks,
    local_index,
    head_index,
):
    blk = local_blocks.shape[-1]
    rows, arcs = arc_flows.shape
    arc_blks, touches = local_index.shape
    node_blks = node_duals.shape[1] // blk
    net = lax.axis_size("net")
    ns = lax.axis_size("scen")
    nx = net // NZ
    slots = NZ * SLOT
    smem = pl.BlockSpec(memory_space=pltpu.SMEM)
    vmem = pl.BlockSpec(memory_space=pltpu.VMEM)
    hbm = pl.BlockSpec(memory_space=pl.ANY)

    def floats(*shape):
        return jax.ShapeDtypeStruct(shape, F32)

    def panel(*lead):
        return pltpu.VMEM((*lead, rows, blk), BF16)

    def wide(*lead):
        return pltpu.VMEM((*lead, rows, blk), F32)

    def row(*lead):
        return pltpu.VMEM((*lead, 1, blk), F32)

    dma = pltpu.SemaphoreType.DMA
    groups = len(GROUPS)
    scratch = (
        [
            pltpu.VMEM(local_blocks.shape, BF16),
            pltpu.VMEM(head_blocks.shape, BF16),
            pltpu.VMEM(arc_flows.shape, F32),
            pltpu.VMEM(demand.shape, F32),
        ]
        + [panel(node_blks)] * NZ
        + [
            pltpu.VMEM((nx, nx * slots), jnp.int32),
            pltpu.SMEM((nx, nx * slots), jnp.int32),
            pltpu.SMEM((4, 128), jnp.int32),
            wide(arc_blks),
            panel(arc_blks),
            wide(arc_blks * touches + 1),
            wide(nx * slots + 1),
            wide(nx * slots),
            wide(slots),
            panel(nx * slots),
            panel(nx * slots),
            panel(nx * slots),
            panel(nx * slots),
            panel(4, node_blks),
            panel(4, node_blks),
            panel(4, node_blks),
            panel(4, node_blks),
            row(),
            row(),
            row(),
            row(ROUNDS, nx),
            row(ROUNDS, NZ),
            row(ROUNDS, ns),
            dma((8,)),
        ]
        + [dma((nx - 1,))] * 2
        + [dma((8 * PARTS,))] * 2
        + [dma((groups * (nx - 1),))] * 4
        + [dma((8 * PARTS,))] * 2
        + [dma((ROUNDS * (nx - 1),))] * 2
        + [dma((ROUNDS * (NZ - 1),))] * 2
        + [dma((ROUNDS * (ns - 1),))] * 2
    )
    own, want = pl.pallas_call(
        functools.partial(table_kernel, nx, node_blks),
        out_shape=(
            jax.ShapeDtypeStruct((8, blk), jnp.int32),
            jax.ShapeDtypeStruct((1, nx * slots), jnp.int32),
        ),
        in_specs=[vmem, vmem],
        out_specs=(vmem, vmem),
        name="tables",
    )(head_index.reshape(1, arc_blks), local_index.T)
    results = pl.pallas_call(
        functools.partial(main_kernel, nx, ns, float(rows * ns), float(arcs * net)),
        out_shape=(floats(rows, arcs), floats(*node_duals.shape), floats(1, rows), floats(1, rows), floats(1, 1)),
        in_specs=[hbm, hbm, hbm, vmem, vmem, vmem, vmem, hbm, hbm, smem, smem, vmem],
        out_specs=(hbm, vmem, vmem, vmem, vmem),
        scratch_shapes=scratch,
        compiler_params=pltpu.CompilerParams(
            collective_id=0, has_side_effects=True, vmem_limit_bytes=67043328
        ),
        name="rounds",
    )(
        node_duals,
        arc_flows,
        demand,
        arc_costs.reshape(arc_blks, blk),
        excess.reshape(1, rows),
        risk_duals.reshape(1, rows),
        threshold.reshape(1, 1),
        local_blocks,
        head_blocks,
        local_index.T,
        own,
        want,
    )
    flows, duals, excess, risk, level = pl.pallas_call(
        finish_kernel,
        out_shape=tuple(floats(*result.shape) for result in results),
        in_specs=[vmem] * 5,
        out_specs=(vmem,) * 5,
        compiler_params=pltpu.CompilerParams(vmem_limit_bytes=67043328),
        name="finish",
    )(*results)
    return flows, duals, excess.reshape(-1), risk.reshape(-1), level.reshape(-1)


def solution(mesh):
    placed = (
        P("scen", "net"),
        P("scen", "net"),
        P("scen", "net"),
        P("scen"),
        P("scen"),
        P(),
        P("net"),
        P("net", None, None, None),
        P("net", None, None),
        P("net", None),
        P("net"),
    )
    return jax.shard_map(
        per_device,
        mesh=mesh,
        in_specs=placed,
        out_specs=(P("scen", "net"), P("scen", "net"), P("scen"), P("scen"), P()),
        check_vma=False,
    )
```

```python
import functools

import jax
import jax.numpy as jnp
from jax import lax
from jax.experimental import pallas as pl
from jax.experimental.pallas import tpu as pltpu
from jax.sharding import PartitionSpec as P

ROUNDS = 3
NZ = 8
SLOT = 4
PRIMAL = 0.5
DUAL = 0.5
RISK = 1.0
TAIL = 2.0
MESH = pl.DeviceIdType.MESH
NT = (((1,), (1,)), ((), ()))
F32 = jnp.float32
BF16 = jnp.bfloat16
ORDER = (4, 3, 5, 2, 6, 1, 7, 0)
GROUPS = ((0, 1), (1, 2), (3, 2), (5, 2), (7, 1))
PARTS = 4
TURNS = ((0, 1, 2, 3), (2, 3, 0, 1))


def halves(n):
    return n.bit_length() - 1


def table_kernel(nx, node_blks, owner_vec, index_vec, own_rows, want_vec):
    touches, arc_blks = index_vec.shape
    blk = own_rows.shape[1]
    slots = NZ * SLOT
    me = lax.axis_index("net")
    x, z = me // NZ, me % NZ

    def count_of(mask, axis):
        return jnp.sum(jnp.where(mask, 1.0, 0.0), axis=axis, keepdims=True).astype(jnp.int32)

    def upright(row):
        n = row.shape[1]
        eye = lax.broadcasted_iota(jnp.int32, (n, n), 0) == lax.broadcasted_iota(jnp.int32, (n, n), 1)
        wide = jnp.broadcast_to(row.astype(F32), (n, n))
        return jnp.sum(jnp.where(eye, wide, 0.0), axis=1, keepdims=True).astype(jnp.int32)

    def highest(mask, value):
        return jnp.max(jnp.where(mask, value, 0.0), axis=0, keepdims=True)

    def place(heads):
        dev = lax.shift_right_logical(heads, halves(node_blks))
        e = (x - lax.shift_right_logical(dev, halves(NZ)) + nx) & (nx - 1)
        o = (z - (dev & (NZ - 1)) + NZ) & (NZ - 1)
        w = jnp.where(o >= 4, 2 * (o - 4), 7 - 2 * o)
        return dev, e * slots + w * SLOT

    square = (arc_blks, arc_blks)
    upper = lax.broadcasted_iota(jnp.int32, square, 0) < lax.broadcasted_iota(jnp.int32, square, 1)
    lower = lax.broadcasted_iota(jnp.int32, square, 0) > lax.broadcasted_iota(jnp.int32, square, 1)
    equal = lax.broadcasted_iota(jnp.int32, square, 0) == lax.broadcasted_iota(jnp.int32, square, 1)
    heads = owner_vec[...]
    heads_up = upright(heads)
    dev, base = place(heads)
    dev_up, base_up = place(heads_up)
    same = dev_up == dev
    pos = base + jnp.minimum(count_of(same & upper, 0), SLOT - 1)
    pos_up = base_up + jnp.minimum(count_of(same & lower, 1), SLOT - 1)
    flat = (arc_blks, nx * slots)
    filled = pos_up == lax.broadcasted_iota(jnp.int32, flat, 1)
    arc_number = lax.broadcasted_iota(jnp.int32, flat, 0).astype(F32)
    inside_up = (heads_up & (node_blks - 1)).astype(F32)
    arcs = highest(filled, arc_number)
    want = node_blks - highest(filled, node_blks - inside_up).astype(jnp.int32)
    want_vec[...] = want
    own_rows[...] = jnp.zeros_like(own_rows)
    own_rows[0:1, 0:arc_blks] = pos
    own_rows[1:2, :] = arcs.astype(jnp.int32)
    own_rows[7:8, :] = want
    step_up = lax.broadcasted_iota(jnp.int32, square, 0).astype(F32) * touches
    column = [upright(index_vec[k : k + 1, :]) for k in range(touches)]
    final = jnp.zeros((1, blk), F32)
    for k in range(touches):
        row = index_vec[k : k + 1, :]
        found = jnp.zeros((1, arc_blks), F32)
        for q in range(touches):
            before = (upper | equal) if q < k else upper
            found = jnp.maximum(found, highest((column[q] == row) & before, step_up + (q + 1)))
        own_rows[2 + k : 3 + k, 0:arc_blks] = found.astype(jnp.int32)
        wide = (arc_blks, blk)
        named = column[k] == lax.broadcasted_iota(jnp.int32, wide, 1)
        final = jnp.maximum(
            final, highest(named, lax.broadcasted_iota(jnp.int32, wide, 0).astype(F32) * touches + (k + 1))
        )
    own_rows[2 + touches : 3 + touches, :] = final.astype(jnp.int32)


def main_kernel(
    nx,
    ns,
    scen_total,
    arc_total,
    duals_hbm,
    flows_hbm,
    demand_hbm,
    cost_ref,
    excess_in,
    risk_in,
    level_in,
    local_hbm,
    head_hbm,
    index_ref,
    own_tab,
    want_vec,
    flows_out,
    duals_ref,
    excess_out,
    risk_out,
    level_out,
    local_ref,
    head_ref,
    flows_ref,
    demand_ref,
    c0, c1, c2, c3, c4, c5, c6, c7,
    ask_vec,
    ask_ref,
    ask_tab,
    pull_ref,
    panel_ref,
    seg_ref,
    segx_ref,
    hp_ref,
    own_ref,
    x_in,
    x_out,
    fx_in,
    fx_out,
    sl_ref,
    sr_ref,
    ll_ref,
    rr_ref,
    excess_ref,
    risk_ref,
    level_ref,
    lossx,
    lossz,
    scen_rows,
    load_sem,
    ask_send, ask_recv,
    ag_send, ag_recv,
    x_send, x_recv,
    f_send, f_recv,
    r_send, r_recv,
    lx_send, lx_recv,
    lz_send, lz_recv,
    sc_send, sc_recv,
):
    chunks = (c0, c1, c2, c3, c4, c5, c6, c7)
    touches, arc_blks = index_ref.shape
    rows = panel_ref.shape[1]
    blk = panel_ref.shape[2]
    node_blks = c0.shape[0]
    part_blks = node_blks // PARTS
    slots = NZ * SLOT
    me = lax.axis_index("net")
    scen = lax.axis_index("scen")
    x, z = me // NZ, me % NZ

    def x_peer(e):
        return {"net": lax.rem(x + e, nx) * NZ + z}

    def z_peer(d):
        return {"net": x * NZ + lax.rem(z + d, NZ)}

    def s_peer(d):
        return {"scen": lax.rem(scen + d, ns)}

    def remote(src, dst, send, recv, device):
        return pltpu.make_async_remote_copy(
            src_ref=src, dst_ref=dst, send_sem=send, recv_sem=recv, device_id=device, device_id_type=MESH
        )

    def columns(b):
        return pl.ds(pl.multiple_of(b * blk, blk), blk)

    def part(h):
        return pl.ds(h * part_blks, part_blks)

    def ag_copy(direction, step, h):
        n = step if direction == 0 else (NZ - step)
        src = chunks[step - 1] if direction == 0 else chunks[(NZ - step + 1) % NZ]
        i = (direction * 4 + step - 1) * PARTS + h
        return remote(
            src.at[part(h)], chunks[n].at[part(h)], ag_send.at[i], ag_recv.at[i], z_peer(1 if direction == 0 else NZ - 1)
        )

    def x_copy(g, e):
        first, count = GROUPS[g]
        i = g * (nx - 1) + e - 1
        return remote(
            x_out.at[pl.ds(e * slots + first * SLOT, count * SLOT)],
            x_in.at[pl.ds(e * slots + first * SLOT, count * SLOT)],
            x_send.at[i], x_recv.at[i], x_peer(e),
        )

    def f_copy(g, e):
        first, count = GROUPS[g]
        i = g * (nx - 1) + e - 1
        return remote(
            fx_out.at[pl.ds(e * slots + first * SLOT, count * SLOT)],
            fx_in.at[pl.ds(e * slots + first * SLOT, count * SLOT)],
            f_send.at[i], f_recv.at[i], x_peer(nx - e),
        )

    def rs_copy(direction, step, h):
        src = (sl_ref if direction == 0 else sr_ref).at[step - 1]
        dst = (ll_ref if direction == 0 else rr_ref).at[step - 1]
        i = (direction * 4 + step - 1) * PARTS + h
        return remote(
            src.at[part(h)], dst.at[part(h)], r_send.at[i], r_recv.at[i], z_peer(NZ - 1 if direction == 0 else 1)
        )

    def lx_copy(r, e):
        i = r * (nx - 1) + e - 1
        return remote(lossx.at[r, x], lossx.at[r, x], lx_send.at[i], lx_recv.at[i], x_peer(e))

    def lz_copy(r, d):
        i = r * (NZ - 1) + d - 1
        return remote(lossz.at[r, z], lossz.at[r, z], lz_send.at[i], lz_recv.at[i], z_peer(d))

    def sc_copy(r, d):
        i = r * (ns - 1) + d - 1
        return remote(scen_rows.at[r, scen], scen_rows.at[r, scen], sc_send.at[i], sc_recv.at[i], s_peer(d))

    def ask_copy(e):
        return remote(want_vec, ask_vec.at[pl.ds(e, 1)], ask_send.at[e - 1], ask_recv.at[e - 1], x_peer(nx - e))

    def start_ring():
        for turn in range(PARTS):
            ag_copy(0, 1, TURNS[0][turn]).start()
            ag_copy(1, 1, TURNS[1][turn]).start()

    loads = [
        pltpu.make_async_copy(src, dst, load_sem.at[i])
        for i, (src, dst) in enumerate(
            (
                (duals_hbm, duals_ref),
                (local_hbm, local_ref),
                (head_hbm, head_ref),
                (flows_hbm, flows_ref),
                (demand_hbm, demand_ref),
            )
        )
    ]
    for load in loads:
        load.start()
    barrier = pltpu.get_barrier_semaphore()
    peers = (
        [x_peer(e) for e in range(1, nx)] + [z_peer(d) for d in range(1, NZ)] + [s_peer(d) for d in range(1, ns)]
    )
    for peer in peers:
        pl.semaphore_signal(barrier, inc=1, device_id=peer, device_id_type=MESH)
    lane = lax.broadcasted_iota(jnp.int32, (rows, blk), 1)
    diagonal = lax.broadcasted_iota(jnp.int32, (rows, blk), 0) == lane
    real = lax.broadcasted_iota(jnp.int32, (1, blk), 1) < rows
    excess_ref[...] = jnp.zeros_like(excess_ref)
    risk_ref[...] = jnp.zeros_like(risk_ref)
    excess_ref[:, 0:rows] = excess_in[...]
    risk_ref[:, 0:rows] = risk_in[...]
    level_ref[...] = jnp.broadcast_to(level_in[...], level_ref.shape)
    seg_ref[0] = jnp.zeros((rows, blk), F32)
    segx_ref[0] = jnp.zeros((rows, blk), F32)

    loads[0].wait()
    for b in range(node_blks):
        c0[b] = duals_ref[:, b * blk : (b + 1) * blk].astype(BF16)
    pl.semaphore_wait(barrier, len(peers))
    for e in range(1, nx):
        ask_copy(e).start()
    start_ring()

    for e in range(1, nx):
        ask_copy(e).wait_recv()
    to_scalar = pltpu.make_async_copy(ask_vec, ask_ref, load_sem.at[5])
    to_scalar.start()
    to_scalar.wait()
    for e in range(1, nx):
        ask_copy(e).wait_send()

    def chain_tables(w, _):
        places = [q // SLOT * slots + w * SLOT + q % SLOT for q in range(nx * SLOT)]
        named = [
            own_tab[touches + 3, i] if q < SLOT else ask_ref[q // SLOT, i] for q, i in enumerate(places)
        ]
        for q, i in enumerate(places):
            found = jnp.int32(0)
            for p in range(q):
                found = jnp.where(named[p] == named[q], places[p] + 1, found)
            ask_tab[0, i] = found
        for b in range(node_blks):
            found = jnp.int32(0)
            for q, i in enumerate(places):
                found = jnp.where(named[q] == b, i + 1, found)
            ask_tab[1, w * node_blks + b] = found
        return 0

    for load in loads[1:]:
        load.wait()

    def pull_local(first, count):
        def body(i, _):
            j = first + i
            total = jnp.zeros((rows, blk), F32)
            for k in range(touches):
                total += lax.dot_general(
                    c0[index_ref[k, j]], local_ref[j, k], NT, preferred_element_type=F32
                )
            pull_ref[j] = total
            return 0

        lax.fori_loop(0, count, body, 0, unroll=min(4, count))

    def push_local(first, count):
        def body(i, _):
            j = first + i
            v = panel_ref[j]
            for k in range(touches):
                term = jnp.dot(v, local_ref[j, k], preferred_element_type=F32)
                seg_ref[j * touches + k + 1] = term + seg_ref[own_tab[2 + k, j]]
            return 0

        lax.fori_loop(0, count, body, 0, unroll=min(4, count))

    def answer_group(g):
        first, count = GROUPS[g]
        for e in range(nx):
            for w in range(first, first + count):
                chunk = chunks[ORDER[w]]
                for s in range(SLOT):
                    i = e * slots + w * SLOT + s
                    named = own_tab[touches + 3, i] if e == 0 else ask_ref[e, i]
                    (x_in if e == 0 else x_out)[i] = chunk[jnp.minimum(named, node_blks - 1)]
            if e > 0:
                x_copy(g, e).start()

    def pull_heads(g):
        first, count = GROUPS[g]

        def body(e, _):
            for s in range(count * SLOT):
                i = e * slots + first * SLOT + s
                hp_ref[i] = lax.dot_general(x_in[i], head_ref[own_tab[1, i]], NT, preferred_element_type=F32)
            return 0

        for e in range(1, nx):
            x_copy(g, e).wait_recv()
        lax.fori_loop(0, nx, body, 0, unroll=nx if g == 0 else 1)

    def push_heads(g):
        first, count = GROUPS[g]

        def term(e, s):
            j = own_tab[1, e * slots + first * SLOT + s]
            return jnp.dot(panel_ref[j], head_ref[j], preferred_element_type=F32)

        def body(e, _):
            for s in range(count * SLOT):
                fx_out[e * slots + first * SLOT + s] = term(e, s).astype(BF16)
            return 0

        lax.fori_loop(1, nx, body, 0, unroll=nx - 1 if g == 0 else 1)
        for e in range(1, nx):
            f_copy(g, e).start()
        for s in range(count * SLOT):
            own_ref[first * SLOT + s] = term(0, s)

    def collect(w):
        for q in range(nx * SLOT):
            e = q // SLOT
            i = w * SLOT + q % SLOT
            n = e * slots + i
            value = own_ref[i] if e == 0 else fx_in[n].astype(F32)
            segx_ref[n + 1] = value + segx_ref[ask_tab[0, n]]

    def send_sum(direction, step, h, with_arrived):
        w = ORDER.index(5 - step if direction == 0 else 3 + step)
        dst = sl_ref if direction == 0 else sr_ref
        arrived = ll_ref if direction == 0 else rr_ref
        if with_arrived:
            rs_copy(direction, step - 1, h).wait_recv()
        for b in range(h * part_blks, (h + 1) * part_blks):
            value = segx_ref[ask_tab[1, w * node_blks + b]]
            if with_arrived:
                value = value + arrived[step - 2, b].astype(F32)
            dst[step - 1, b] = value.astype(BF16)
        rs_copy(direction, step, h).start()

    def one_round(r, _):
        scen_rows[r, scen] = risk_ref[...]
        for d in range(1, ns):
            sc_copy(r, d).start()
        piece = arc_blks // 32
        ahead = (arc_blks - 12 * piece) // 2
        after = arc_blks - 12 * piece - ahead
        answer_group(4)
        pull_local(0, ahead)
        done = ahead
        for step in range(1, 4):
            for turn in range(PARTS):
                for direction in range(2):
                    h = TURNS[direction][turn]
                    ag_copy(direction, step, h).wait_recv()
                    if step < 3 or turn < PARTS // 2:
                        ag_copy(direction, step + 1, h).start()
                if turn == PARTS - 1:
                    answer_group(4 - step)
                pull_local(done, piece)
                done += piece
            if step > 1:
                pull_heads(6 - step)
        for turn in range(PARTS // 2):
            for direction in range(2):
                ag_copy(direction, 4, TURNS[direction][turn]).wait_recv()
        answer_group(0)

        @pl.when(r == 0)
        def _():
            lax.fori_loop(0, NZ, chain_tables, 0)

        pull_local(done, after)
        risk_wide = jnp.broadcast_to(
            jnp.sum(jnp.where(diagonal, jnp.broadcast_to(risk_ref[...], (rows, blk)), 0.0), axis=1, keepdims=True),
            (rows, blk),
        )
        for g in (2, 1, 0):
            pull_heads(g)

        def move(i, loss):
            js = [i * 4 + u for u in range(4)]
            pulled = [pull_ref[j] + hp_ref[own_tab[0, j]] for j in js]
            costs = [jnp.broadcast_to(cost_ref[pl.ds(j, 1), :], (rows, blk)) for j in js]
            now = [flows_ref[:, columns(j)] for j in js]
            new = [jnp.maximum(n - PRIMAL * (risk_wide * c - p), 0.0) for n, c, p in zip(now, costs, pulled)]
            bars = [2.0 * v - n for v, n in zip(new, now)]
            for j, v, bar in zip(js, new, bars):
                flows_ref[:, columns(j)] = v
                panel_ref[j] = bar.astype(BF16)
            for c, bar in zip(costs, bars):
                loss = loss + c * bar
            return loss

        loss = lax.fori_loop(0, arc_blks // 4, move, jnp.zeros((rows, blk), F32))
        keep = pltpu.make_async_copy(flows_ref, flows_out, load_sem.at[7])

        @pl.when(r == ROUNDS - 1)
        def _():
            keep.start()

        for g in range(len(GROUPS)):
            push_heads(g)
        wide = jnp.broadcast_to(jnp.sum(loss, axis=1, keepdims=True), (rows, blk))
        lossx[r, x] = jnp.sum(jnp.where(diagonal, wide, 0.0), axis=0, keepdims=True)
        for e in range(1, nx):
            lx_copy(r, e).start()
        for direction in range(2):
            for step in range(1, 5):
                for turn in range(PARTS):
                    if step < 4 or turn < PARTS // 2:
                        ag_copy(direction, step, TURNS[direction][turn]).wait_send()
        for g in range(len(GROUPS)):
            for e in range(1, nx):
                x_copy(g, e).wait_send()
        push_local(0, ahead)

        for e in range(1, nx):
            f_copy(0, e).wait_recv()
        collect(0)
        for turn in range(PARTS // 2):
            for direction in range(2):
                send_sum(direction, 1, TURNS[direction][turn], False)
        for e in range(1, nx):
            lx_copy(r, e).wait_recv()
        total = lossx[r, 0]
        for i in range(1, nx):
            total = total + lossx[r, i]
        lossz[r, z] = total
        for d in range(1, NZ):
            lz_copy(r, d).start()
        done = ahead
        for step in range(2, 5):
            for e in range(1, nx):
                f_copy(step - 1, e).wait_recv()
            collect(2 * step - 3)
            collect(2 * step - 2)
            for turn in range(PARTS):
                for direction in range(2):
                    send_sum(direction, step, TURNS[1 - direction][turn], step > 2 or turn >= PARTS // 2)
                push_local(done, piece)
                done += piece
        for e in range(1, nx):
            f_copy(4, e).wait_recv()
        collect(7)
        push_local(done, after)

        for turn in range(PARTS):
            for direction in range(2):
                rs_copy(direction, 4, TURNS[1 - direction][turn]).wait_recv()
        for b in range(node_blks):
            pushed = (
                seg_ref[own_tab[2 + touches, b]]
                + segx_ref[ask_tab[1, 7 * node_blks + b]]
                + (ll_ref[3, b].astype(F32) + rr_ref[3, b].astype(F32))
            )
            dual = duals_ref[:, b * blk : (b + 1) * blk] + DUAL * (demand_ref[:, b * blk : (b + 1) * blk] - pushed)
            duals_ref[:, b * blk : (b + 1) * blk] = dual
            c0[b] = dual.astype(BF16)
        @pl.when(r < ROUNDS - 1)
        def _():
            start_ring()

        for direction in range(2):
            for step in range(1, 5):
                for turn in range(PARTS):
                    if step > 1 or turn < PARTS // 2:
                        rs_copy(direction, step, TURNS[direction][turn]).wait_send()
        for g in range(len(GROUPS)):
            for e in range(1, nx):
                f_copy(g, e).wait_send()

        for d in range(1, NZ):
            lz_copy(r, d).wait_recv()
        losses = lossz[r, 0]
        for i in range(1, NZ):
            losses = losses + lossz[r, i]
        losses = losses / arc_total
        for d in range(1, ns):
            sc_copy(r, d).wait_recv()
        risk_sum = scen_rows[r, 0]
        for i in range(1, ns):
            risk_sum = risk_sum + scen_rows[r, i]
        mean = jnp.broadcast_to(jnp.sum(risk_sum, axis=1, keepdims=True), (1, blk)) / scen_total
        risk = risk_ref[...]
        excess = excess_ref[...]
        level = level_ref[...]
        excess_new = jnp.maximum(excess - PRIMAL * (TAIL - risk), 0.0)
        level_new = level - PRIMAL * (1.0 - mean)
        excess_bar = 2.0 * excess_new - excess
        level_bar = 2.0 * level_new - level
        risk_new = jnp.maximum(risk + RISK * (losses - excess_bar - level_bar), 0.0)
        excess_ref[...] = excess_new
        level_ref[...] = level_new
        for d in range(1, ns):
            sc_copy(r, d).wait_send()
        for d in range(1, NZ):
            lz_copy(r, d).wait_send()
        for e in range(1, nx):
            lx_copy(r, e).wait_send()
        risk_ref[...] = jnp.where(real, risk_new, 0.0)
        return 0

    lax.fori_loop(0, ROUNDS, one_round, 0)
    pltpu.make_async_copy(flows_ref, flows_out, load_sem.at[7]).wait()
    excess_out[...] = excess_ref[:, 0:rows]
    risk_out[...] = risk_ref[:, 0:rows]
    level_out[...] = level_ref[:, 0:1]


def finish_kernel(*refs):
    for src, dst in zip(refs[:5], refs[5:]):
        dst[...] = src[...]


def per_device(
    arc_flows,
    node_duals,
    demand,
    excess,
    risk_duals,
    threshold,
    arc_costs,
    local_blocks,
    head_blocks,
    local_index,
    head_index,
):
    blk = local_blocks.shape[-1]
    rows, arcs = arc_flows.shape
    arc_blks, touches = local_index.shape
    node_blks = node_duals.shape[1] // blk
    net = lax.axis_size("net")
    ns = lax.axis_size("scen")
    nx = net // NZ
    slots = NZ * SLOT
    smem = pl.BlockSpec(memory_space=pltpu.SMEM)
    vmem = pl.BlockSpec(memory_space=pltpu.VMEM)
    hbm = pl.BlockSpec(memory_space=pl.ANY)

    def floats(*shape):
        return jax.ShapeDtypeStruct(shape, F32)

    def panel(*lead):
        return pltpu.VMEM((*lead, rows, blk), BF16)

    def wide(*lead):
        return pltpu.VMEM((*lead, rows, blk), F32)

    def row(*lead):
        return pltpu.VMEM((*lead, 1, blk), F32)

    dma = pltpu.SemaphoreType.DMA
    groups = len(GROUPS)
    scratch = (
        [
            pltpu.VMEM(local_blocks.shape, BF16),
            pltpu.VMEM(head_blocks.shape, BF16),
            pltpu.VMEM(arc_flows.shape, F32),
            pltpu.VMEM(demand.shape, F32),
        ]
        + [panel(node_blks)] * NZ
        + [
            pltpu.VMEM((nx, nx * slots), jnp.int32),
            pltpu.SMEM((nx, nx * slots), jnp.int32),
            pltpu.SMEM((4, 128), jnp.int32),
            wide(arc_blks),
            panel(arc_blks),
            wide(arc_blks * touches + 1),
            wide(nx * slots + 1),
            wide(nx * slots),
            wide(slots),
            panel(nx * slots),
            panel(nx * slots),
            panel(nx * slots),
            panel(nx * slots),
            panel(4, node_blks),
            panel(4, node_blks),
            panel(4, node_blks),
            panel(4, node_blks),
            row(),
            row(),
            row(),
            row(ROUNDS, nx),
            row(ROUNDS, NZ),
            row(ROUNDS, ns),
            dma((8,)),
        ]
        + [dma((nx - 1,))] * 2
        + [dma((8 * PARTS,))] * 2
        + [dma((groups * (nx - 1),))] * 4
        + [dma((8 * PARTS,))] * 2
        + [dma((ROUNDS * (nx - 1),))] * 2
        + [dma((ROUNDS * (NZ - 1),))] * 2
        + [dma((ROUNDS * (ns - 1),))] * 2
    )
    own, want = pl.pallas_call(
        functools.partial(table_kernel, nx, node_blks),
        out_shape=(
            jax.ShapeDtypeStruct((8, blk), jnp.int32),
            jax.ShapeDtypeStruct((1, nx * slots), jnp.int32),
        ),
        in_specs=[vmem, vmem],
        out_specs=(vmem, vmem),
        name="tables",
    )(head_index.reshape(1, arc_blks), local_index.T)
    results = pl.pallas_call(
        functools.partial(main_kernel, nx, ns, float(rows * ns), float(arcs * net)),
        out_shape=(floats(rows, arcs), floats(*node_duals.shape), floats(1, rows), floats(1, rows), floats(1, 1)),
        in_specs=[hbm, hbm, hbm, vmem, vmem, vmem, vmem, hbm, hbm, smem, smem, vmem],
        out_specs=(hbm, vmem, vmem, vmem, vmem),
        scratch_shapes=scratch,
        compiler_params=pltpu.CompilerParams(
            collective_id=0, has_side_effects=True, vmem_limit_bytes=67043328
        ),
        name="rounds",
    )(
        node_duals,
        arc_flows,
        demand,
        arc_costs.reshape(arc_blks, blk),
        excess.reshape(1, rows),
        risk_duals.reshape(1, rows),
        threshold.reshape(1, 1),
        local_blocks,
        head_blocks,
        local_index.T,
        own,
        want,
    )
    flows, duals, excess, risk, level = pl.pallas_call(
        finish_kernel,
        out_shape=tuple(floats(*result.shape) for result in results),
        in_specs=[vmem] * 5,
        out_specs=(vmem,) * 5,
        compiler_params=pltpu.CompilerParams(vmem_limit_bytes=67043328),
        name="finish",
    )(*results)
    return flows, duals, excess.reshape(-1), risk.reshape(-1), level.reshape(-1)


def solution(mesh):
    placed = (
        P("scen", "net"),
        P("scen", "net"),
        P("scen", "net"),
        P("scen"),
        P("scen"),
        P(),
        P("net"),
        P("net", None, None, None),
        P("net", None, None),
        P("net", None),
        P("net"),
    )
    return jax.shard_map(
        per_device,
        mesh=mesh,
        in_specs=placed,
        out_specs=(P("scen", "net"), P("scen", "net"), P("scen"), P("scen"), P()),
        check_vma=False,
    )
```
